128 devices in a mesh: gy: 8 (over x, core), gz: 16 (over y, z).
Axes of the slice: x: 4, y: 4, z: 4, core: 2. Of those that a mesh axis runs over, the one named last changes fastest.
Arguments:
- offsets: float32 [3, 1048576], P(None, ('gy', 'gz')), may hold values from 0 to 1
- masses: float32 [1048576], P(('gy', 'gz')), may hold values from 0.25 to 4
- velocities: float32 [3, 1048576], P(None, ('gy', 'gz')), may hold values from -5 to 5
- destination: int32 [1048576, 1], P(('gy', 'gz')), may hold values from 0 to 127; in each aligned block of 8192 rows (0 to 8191, 8192 to 16383, ...) at most 128 rows name the same one
- first_weight: bfloat16 [16, 4, 3, 3, 3], replicated, may hold values from -0.625 to 0.625
- first_bias: float32 [16], replicated, may hold values from -3 to 3
- second_weight: bfloat16 [16, 16, 3, 3, 3], replicated, may hold values from -0.3125 to 0.3125
- second_bias: float32 [16], replicated, may hold values from -3 to 3
- cotangent: bfloat16 [16, 64, 128, 128], P(None, 'gy', 'gz'), may hold values from -6 to 6
Outputs:
- refined: bfloat16 [16, 64, 128, 128], P(None, 'gy', 'gz')
- grad_field: float32 [4, 64, 128, 128], P(None, 'gy', 'gz')
- grad_first_weight: float32 [16, 4, 3, 3, 3], replicated
- grad_first_bias: float32 [16], replicated
- grad_second_weight: float32 [16, 16, 3, 3, 3], replicated
- grad_second_bias: float32 [16], replicated
The draws below stay inside these ranges and needn't reach their ends.
Inputs may be any that keep to these rules, and one draw needn't show every extreme that they name: `destination`: in the rows of one device (aligned blocks of 8192 rows) no block number is named by more than 128 rows, and some block number is named by exactly 128.
All inputs are finite; a program needn't handle non-finite values.
Results may differ from the reference program's by a relative error of at most 0.009.
Values may be sent and summed in bfloat16 or wider, within the bound.
A program may use at most 192 MiB of HBM per device.

```python
import math
import jax
import jax.numpy as jnp
import numpy as np
from jax import lax

CH = 16
C_IN = 4
BY = 8
BZ = 8
NXW = 128
NY = 64
NZ = 128
PART_DEV = 8192
CAP = 128
PARTICLES = 1048576
N_GZ = 16
DEVICES = 128


def level_of(stream_key, extent, cuts, smallest, high):
    loudness = 1.0
    for dim, parts in cuts:
        draws = jax.random.uniform(jax.random.fold_in(jax.random.fold_in(stream_key, 6), dim), (parts,), jnp.float32, smallest / len(cuts), high / len(cuts))
        loudness = loudness * jnp.repeat(jnp.exp(draws), extent[dim] // parts).reshape((-1,) + (1,) * (len(extent) - 1 - dim))
    return loudness


def deal_out(stream_key, own, number, rows, amount, top, reach, skew):
    sequence = jax.random.permutation(stream_key, amount)
    packed, ordinary = load_shares(amount, rows * top, reach, skew, True), load_shares(amount, rows * top, reach, skew, False)
    places = jnp.arange(amount)

    def named(sizes, turn):
        used = int((sizes > 0).sum())
        fixed = max(1, used // 4)
        shifted = fixed + (places - fixed + turn * (used - fixed)) % max(1, amount - fixed)
        return jnp.zeros((amount,), jnp.int32).at[sequence[jnp.where(places < fixed, places, shifted)]].set(jnp.asarray(sizes, jnp.int32))

    sizes = jnp.where(number % 4 == 0, named(packed, number // 4), named(ordinary, number - number // 4 - 1))
    mixed = jax.random.permutation(jax.random.fold_in(own, 3), amount)
    donor, taker = mixed[0:amount // 2 * 2:2], mixed[1:amount // 2 * 2:2]
    room = jnp.minimum(sizes[donor] - 1, reach - sizes[taker]) // 2
    room = jnp.where((donor == sequence[0]) | (taker == sequence[0]) | (sizes[taker] == 0), 0, jnp.maximum(room, 0))
    shifted = jax.random.randint(jax.random.fold_in(own, 4), (amount // 2,), 0, 1 << 20) % (room + 1)
    sizes = sizes.at[donor].add(-shifted).at[taker].add(shifted)
    members = jnp.searchsorted(jnp.cumsum(sizes), jnp.arange(rows * top), side="right").astype(jnp.int32)
    table = members.reshape(top, rows).T
    table = table[jax.random.permutation(jax.random.fold_in(own, 1), rows)]
    turn = jax.random.randint(jax.random.fold_in(own, 2), (rows, 1), 0, top)
    return jnp.take_along_axis(table, (jnp.arange(top)[None, :] + turn) % top, axis=1)


def load_shares(count, total, most, slope, full):
    weights = [(1 << 20) // math.isqrt(standing ** slope) + 1 for standing in range(1, count + 1)]
    largest = most if full else min(most, max(-(-total // count), total * weights[0] // sum(weights)))
    least = 1 if total - largest >= count - 1 else 0
    counts, spare = [largest] + [least] * (count - 1), total - largest - least * (count - 1)
    while spare > 0:
        movable = [i for i in range(1, count) if counts[i] < largest] or [i for i in range(1, count) if counts[i] < most]
        pool, left = sum([weights[i] for i in movable]), spare
        for i in movable:
            addition = min(most - counts[i], max(1, left * weights[i] // pool), spare)
            counts[i] = counts[i] + addition
            spare = spare - addition
    return np.array(counts)


def scatter_about(key, extent, deviation, bound, cuts=(), held_as=jnp.bfloat16):
    result = deviation * jax.random.normal(key, extent, jnp.float32)
    if cuts:
        result = result * level_of(key, extent, cuts, -0.22, 0.18)
    return jnp.clip(result, -bound, bound).astype(held_as)


def setup_inputs(seed: int = 0) -> dict:
    arg_keys = jax.random.split(jax.random.key(seed), 10)
    offsets = jnp.clip(1.0 * jax.random.uniform(arg_keys[0], (3, PARTICLES), jnp.float32) ** level_of(arg_keys[0], (3, PARTICLES), ((1, 128),), -0.2, 0.2), 0.0, 1.0)
    masses = jnp.clip(jnp.exp(math.log(4.0) - 2.7725887 * jax.random.uniform(arg_keys[1], (PARTICLES,), jnp.float32) ** level_of(arg_keys[1], (PARTICLES,), ((0, 128),), -0.2, 0.2)), 0.25, 4.0)
    velocities = scatter_about(arg_keys[2], (3, PARTICLES), 1.0, 5.0, ((1, 128),), jnp.float32)
    destination_keys = jax.random.split(jax.random.fold_in(arg_keys[3], 1), PARTICLES // PART_DEV)
    destination_turns = jax.random.permutation(jax.random.fold_in(arg_keys[3], 3), PARTICLES // PART_DEV)
    destination = jax.vmap(lambda own, number: deal_out(jax.random.fold_in(arg_keys[3], 2), own, number, PART_DEV, DEVICES, 1, CAP, 1))(destination_keys, destination_turns).reshape((PARTICLES, 1))
    first_weight = scatter_about(arg_keys[4], (CH, C_IN, 3, 3, 3), (27 * C_IN) ** -0.5, 0.625)
    first_bias = scatter_about(arg_keys[5], (CH,), 0.5, 3.0, (), jnp.float32)
    second_weight = scatter_about(arg_keys[6], (CH, CH, 3, 3, 3), (27 * CH) ** -0.5, 0.3125)
    second_bias = scatter_about(arg_keys[7], (CH,), 0.5, 3.0, (), jnp.float32)
    cotangent = scatter_about(arg_keys[8], (CH, NY, NZ, NXW), 1.0, 6.0, ((1, 8), (2, 16)))
    return dict(offsets=offsets, masses=masses, velocities=velocities, destination=destination, first_weight=first_weight, first_bias=first_bias, second_weight=second_weight, second_bias=second_bias, cotangent=cotangent)


def cell_split(coord, span):
    position = coord * span
    cell = jnp.minimum(jnp.floor(position).astype(jnp.int32), span - 1)
    frac = position - cell.astype(position.dtype)
    return (cell, frac)

def deposit_cloud(offsets, masses, velocities, base_y, base_z, span_y, span_z, span_x, grid_y, grid_z, grid_x):
    cell_y, frac_y = cell_split(offsets[0], span_y)
    cell_z, frac_z = cell_split(offsets[1], span_z)
    cell_x, frac_x = cell_split(offsets[2], span_x)
    charges = jnp.concatenate([masses[None, :], masses[None, :] * velocities], axis=0)
    total = jnp.zeros((charges.shape[0], grid_y * grid_z * grid_x), masses.dtype)
    for step_y in range(2):
        weight_y = frac_y if step_y else 1.0 - frac_y
        for step_z in range(2):
            weight_z = frac_z if step_z else 1.0 - frac_z
            for step_x in range(2):
                weight_x = frac_x if step_x else 1.0 - frac_x
                index = ((base_y + cell_y + step_y) * grid_z + (base_z + cell_z + step_z)) * grid_x + cell_x + step_x
                total = total.at[:, index].add(charges * (weight_y * weight_z * weight_x)[None, :])
    return total.reshape(charges.shape[0], grid_y, grid_z, grid_x)

def conv_valid(source, kernel):
    return lax.conv_general_dilated(source[None], kernel, (1, 1, 1), 'VALID', dimension_numbers=('NCDHW', 'OIDHW', 'NCDHW'), preferred_element_type=jnp.float32)[0]

def padded32(field):
    return jnp.pad(field.astype(jnp.float32), ((0, 0), (1, 1), (1, 1), (1, 1)))

def flipped(kernel):
    return jnp.flip(kernel, (2, 3, 4)).transpose(1, 0, 2, 3, 4)

def dsilu(value):
    sig = jax.nn.sigmoid(value)
    return sig * (1.0 + value * (1.0 - sig))

def kernel_grad(source, delta, kernel):
    source_pad = padded32(source)
    _, pull = jax.vjp(lambda weights: conv_valid(source_pad, weights), kernel.astype(jnp.float32))
    return pull(delta.astype(jnp.float32))[0]

def reference(offsets, masses, velocities, destination, first_weight, first_bias, second_weight, second_bias, cotangent):
    target = destination[:, 0]
    base_y = target // N_GZ * BY
    base_z = target % N_GZ * BZ
    whole = deposit_cloud(offsets, masses, velocities, base_y, base_z, BY, BZ, NXW, NY + 1, NZ + 1, NXW + 1)
    density = whole[:, :NY, :NZ, :NXW].astype(jnp.bfloat16)
    pre_one = conv_valid(padded32(density), first_weight.astype(jnp.float32)) + first_bias[:, None, None, None]
    active = jax.nn.silu(pre_one).astype(jnp.bfloat16)
    pre_two = conv_valid(padded32(active), second_weight.astype(jnp.float32)) + second_bias[:, None, None, None]
    refined = jax.nn.silu(pre_two).astype(jnp.bfloat16)
    delta_two = (cotangent.astype(jnp.float32) * dsilu(pre_two)).astype(jnp.bfloat16)
    back_one = conv_valid(padded32(delta_two), flipped(second_weight).astype(jnp.float32))
    delta_one = (back_one * dsilu(pre_one)).astype(jnp.bfloat16)
    grad_field = conv_valid(padded32(delta_one), flipped(first_weight).astype(jnp.float32))
    scale = 1.0 / jnp.sqrt(jnp.float32(NY * NZ * NXW))
    grad_second_weight = kernel_grad(active, delta_two, second_weight) * scale
    grad_second_bias = lax.optimization_barrier(jnp.sum(delta_two.astype(jnp.float32), axis=(1, 2, 3))) * scale
    grad_first_weight = kernel_grad(density, delta_one, first_weight) * scale
    grad_first_bias = lax.optimization_barrier(jnp.sum(delta_one.astype(jnp.float32), axis=(1, 2, 3))) * scale
    return (refined, grad_field, grad_first_weight, grad_first_bias, grad_second_weight, grad_second_bias)
```

```python
import functools
import math

import jax
import jax.numpy as jnp
from jax import lax
from jax.experimental import pallas as pl
from jax.experimental.pallas import tpu as pltpu
from jax.sharding import PartitionSpec as P

F32 = jnp.float32
BF = jnp.bfloat16
MESH = pl.DeviceIdType.MESH
NT = (((1,), (1,)), ((), ()))
TN = (((0,), (0,)), ((), ()))
NN = (((1,), (0,)), ((), ()))
VMEM = pl.BlockSpec(memory_space=pltpu.VMEM)
SMEM = pl.BlockSpec(memory_space=pltpu.SMEM)
LIMIT = 62 * 1024 * 1024


def dot(a, b, dims=NN):
    return lax.dot_general(a, b, dims, preferred_element_type=F32)


def iota(shape, dim):
    return lax.broadcasted_iota(jnp.int32, shape, dim)


def halves(value):
    high = value.astype(BF)
    return high, (value - high.astype(F32)).astype(BF)


def pack_body(chunk, off, mass, vel, dest, out, acc):
    blocks, _, slots = out.shape
    count = off.shape[1]
    rows = iota((blocks, chunk), 0)
    ranks = iota((slots, chunk), 0).astype(F32)
    before = (iota((chunk, chunk), 0) < iota((chunk, chunk), 1)).astype(F32).astype(BF)
    acc[...] = jnp.zeros_like(acc)

    def step(k, base):
        here = pl.ds(pl.multiple_of(k * chunk, chunk), chunk)
        hot = (rows == dest[:, here]).astype(F32)
        hot16 = hot.astype(BF)
        earlier = dot(hot16, before) + base
        rank = jnp.sum(hot * earlier, axis=0, keepdims=True)
        place = (ranks == rank).astype(F32).astype(BF)
        spot = off[:, here]
        m = mass[:, here]
        v = vel[:, here]
        planes = (
            halves(spot[2:3] * 128.0)
            + halves(spot[0:1] * 8.0)
            + halves(spot[1:2] * 8.0)
            + (m.astype(BF), (m * v[0:1]).astype(BF), (m * v[1:2]).astype(BF), (m * v[2:3]).astype(BF))
        )
        spread = jnp.concatenate([place * plane for plane in planes], axis=0)
        acc[...] += dot(hot16, spread, NT)
        return base + jnp.sum(hot, axis=1, keepdims=True)

    lax.fori_loop(0, count // chunk, step, jnp.zeros((blocks, 1), F32))

    def plane(i):
        return acc[:, i * slots : (i + 1) * slots]

    for i in range(3):
        out[:, i, :] = plane(2 * i) + plane(2 * i + 1)
    out[:, 3, :] = jnp.zeros((blocks, slots), F32)
    for i in range(4):
        out[:, 4 + i, :] = plane(6 + i)


def pack(off, mass, vel, dest, blocks, slots):
    return pl.pallas_call(
        functools.partial(pack_body, 512),
        out_shape=jax.ShapeDtypeStruct((blocks, 8, slots), F32),
        in_specs=[VMEM] * 4,
        out_specs=VMEM,
        scratch_shapes=[pltpu.VMEM((blocks, 10 * slots), F32)],
        compiler_params=pltpu.CompilerParams(vmem_limit_bytes=LIMIT),
        name="pack",
    )(off, mass, vel, dest)


GROUP = 4


def hat(grid, at):
    return jnp.maximum(1.0 - jnp.abs(grid - at), 0.0)


def deposit_body(got, out, acc):
    sources = got.shape[0]
    xs = iota((128, 128), 0).astype(F32)
    zs = (iota((40, 128), 0) >> 2).astype(F32)
    ys = iota((16, 128), 0).astype(F32)
    upper = iota((8, 128), 0) >= 4
    acc[...] = jnp.zeros_like(acc)

    def factors(s):
        t = got[s]
        wx = hat(xs, t[0:1]).astype(BF)
        q = jnp.where(upper, t, pltpu.roll(t, 4, 0))
        wzq = hat(zs, t[2:3]) * jnp.concatenate([q] * 5, axis=0)
        wy = hat(ys, t[1:2])
        return wx, jnp.concatenate([wzq * wy[y : y + 1] for y in range(9)], axis=0).astype(BF)

    def step(k, carry):
        pairs = [factors(k * GROUP + i) for i in range(GROUP)]
        right = jnp.concatenate([p[0] for p in pairs], axis=1)
        left = jnp.concatenate([p[1] for p in pairs], axis=1)
        acc[...] += dot(left, right, NT)
        return carry

    lax.fori_loop(0, sources // GROUP, step, 0)
    for y in range(9):
        out[y] = acc[y * 40 : (y + 1) * 40]


def deposit(got):
    return pl.pallas_call(
        deposit_body,
        out_shape=jax.ShapeDtypeStruct((9, 40, 128), F32),
        in_specs=[VMEM],
        out_specs=VMEM,
        scratch_shapes=[pltpu.VMEM((360, 128), F32)],
        compiler_params=pltpu.CompilerParams(vmem_limit_bytes=LIMIT),
        name="deposit",
    )(got)


Y_PART = {1: (4, 5), 0: (0, 9), -1: (0, 4)}
Z_PART = {1: (16, 24), 0: (0, 40), -1: (0, 16)}
AROUND = [(a, b) for a in (1, 0, -1) for b in (1, 0, -1) if (a, b) != (0, 0)]
C_FROM = {1: (6, 2), 0: (0, 8), -1: (0, 2)}
C_INTO = {1: 0, 0: 2, -1: 10}


def halo_body(ny, nz, part, cot, *rest):
    got, cext = rest[:8], rest[8]
    send, receive, own = rest[9:]
    me_y, me_z = lax.axis_index("gy"), lax.axis_index("gz")
    barrier = pltpu.get_barrier_semaphore()

    def device(a, b):
        return (lax.rem(me_y + a + ny, ny), lax.rem(me_z + b + nz, nz))

    for a, b in AROUND:
        pl.semaphore_signal(barrier, inc=1, device_id=device(a, b), device_id_type=MESH)
    mine = pltpu.make_async_copy(cot, cext.at[pl.ds(2, 8), pl.ds(2, 8)], own)
    mine.start()
    pl.semaphore_wait(barrier, 8)
    copies = []
    for i, (a, b) in enumerate(AROUND):
        copies.append(
            pltpu.make_async_remote_copy(
                src_ref=part.at[pl.ds(*Y_PART[a]), pl.ds(*Z_PART[b])],
                dst_ref=got[i],
                send_sem=send.at[i],
                recv_sem=receive.at[i],
                device_id=device(a, b),
                device_id_type=MESH,
            )
        )
        copies.append(
            pltpu.make_async_remote_copy(
                src_ref=cot.at[pl.ds(*C_FROM[a]), pl.ds(*C_FROM[b])],
                dst_ref=cext.at[pl.ds(C_INTO[a], C_FROM[a][1]), pl.ds(C_INTO[b], C_FROM[b][1])],
                send_sem=send.at[8 + i],
                recv_sem=receive.at[8 + i],
                device_id=device(a, b),
                device_id_type=MESH,
            )
        )
    for c in copies:
        c.start()
    mine.wait()
    for c in copies:
        c.wait()


def halo(part, cot, ny, nz):
    return pl.pallas_call(
        functools.partial(halo_body, ny, nz),
        out_shape=[jax.ShapeDtypeStruct((Y_PART[a][1], Z_PART[b][1], 128), F32) for a, b in AROUND]
        + [jax.ShapeDtypeStruct((12, 12, 16, 128), BF)],
        in_specs=[VMEM] * 2,
        out_specs=[VMEM] * 9,
        scratch_shapes=[
            pltpu.SemaphoreType.DMA((16,)),
            pltpu.SemaphoreType.DMA((16,)),
            pltpu.SemaphoreType.DMA,
        ],
        compiler_params=pltpu.CompilerParams(collective_id=1, has_side_effects=True),
        name="halo",
    )(part, cot)


def tables_body(w1, w2, t1, t2, t2f, t1f):
    lane256, lane128 = iota((16, 256), 1), iota((16, 128), 1)
    rep16 = ((lane256 & 15) == iota((16, 256), 0)).astype(F32).astype(BF)
    rep4 = ((iota((4, 128), 1) & 3) == iota((4, 128), 0)).astype(F32).astype(BF)
    lane8 = iota((8, 256), 1)

    def tap(y, z, x):
        return (y * 3 + z) * 3 + x

    def back(y, z, x):
        return tap(2 - y, 2 - z, 2 - x)

    taps = [(y, z) for y in range(3) for z in range(3)]
    for x in range(3):
        r2 = {(y, z): dot(w2[tap(y, z, x)], rep16) for y, z in taps}
        r2f = {(y, z): dot(w2[back(y, z, x)], rep16, TN) for y, z in taps}
        r1 = {(y, z): dot(w1[tap(y, z, x)], rep4, TN) for y, z in taps}
        r1f = {
            (y, z): jnp.concatenate([dot(w1[back(y, z, x)], rep16), jnp.zeros((4, 256), F32)], axis=0)
            for y, z in taps
        }
        for oy in range(2):
            for oz in range(2):
                a = jnp.zeros((16, 256), F32)
                b = jnp.zeros((16, 256), F32)
                c = jnp.zeros((8, 256), F32)
                for y, z in taps:
                    block = (oy + y) * 4 + oz + z
                    a = jnp.where((lane256 >> 4) == block, r2[y, z], a)
                    b = jnp.where((lane256 >> 4) == block, r2f[y, z], b)
                    c = jnp.where((lane8 >> 4) == block, r1f[y, z], c)
                row = (x * 4 + oy * 2 + oz) * 16
                t2[row : row + 16] = a.astype(BF)
                t2f[row : row + 16] = b.astype(BF)
                t1f[row // 2 : row // 2 + 8] = c
            for oz in range(4):
                a = jnp.zeros((16, 128), F32)
                for y, z in taps:
                    a = jnp.where((lane128 >> 2) == (oy + y) * 8 + oz + z, r1[y, z], a)
                row = (x * 8 + oy * 4 + oz) * 16
                t1[row : row + 16] = a.astype(BF)


def tables(w1, w2):
    return pl.pallas_call(
        tables_body,
        out_shape=[
            jax.ShapeDtypeStruct((384, 128), BF),
            jax.ShapeDtypeStruct((192, 256), BF),
            jax.ShapeDtypeStruct((192, 256), BF),
            jax.ShapeDtypeStruct((96, 256), F32),
        ],
        in_specs=[VMEM] * 2,
        out_specs=[VMEM] * 4,
        compiler_params=pltpu.CompilerParams(vmem_limit_bytes=LIMIT),
        name="tables",
    )(w1, w2)


def unet_body(
    ny,
    nz,
    pos,
    part,
    bl,
    bo,
    br,
    sl,
    sr,
    al,
    ao,
    ar,
    cext,
    t1,
    t2,
    t2f,
    t1f,
    b1,
    b2,
    refined,
    field,
    sums,
    dens,
    act,
    ds1,
    d2,
    d1,
    g2,
    g1,
    s2,
    s1,
):
    gy, gz = pos[0], pos[1]
    lane = iota((128, 128), 1)
    not_first, not_last = lane > 0, lane < 127

    def from_left(v):
        return jnp.where(not_first[: v.shape[0]], pltpu.roll(v, 1, 1), 0.0)

    def from_right(v):
        return jnp.where(not_last[: v.shape[0]], pltpu.roll(v, 127, 1), 0.0)

    def along_x(v, rows, j):
        cols = slice(j * 128, (j + 1) * 128)
        return from_left(v[:rows, cols]) + v[rows : 2 * rows, cols] + from_right(v[2 * rows :, cols])

    zrow = (iota((80, 128), 0) >> 2) - 5 + gz * 8
    z_inside = (zrow >= 0) & (zrow < nz * 8)

    from_side = (gz > 0).astype(F32)
    from_below = (gy > 0).astype(F32)

    def across(left, own, right):
        return jnp.concatenate(
            [
                left[0:16],
                own[0:8] + left[16:24] * from_side,
                own[8:32],
                right[0:8] + own[32:40],
                right[8:16],
            ],
            axis=0,
        )

    for y in range(16):
        if y < 4:
            slab = across(bl[y], bo[y], br[y])
        elif y < 12:
            slab = across(sl[y - 4], part[y - 4], sr[y - 4])
            if y == 4:
                slab = slab + across(bl[4], bo[4], br[4]) * from_below
        else:
            slab = across(al[y - 12], ao[y - 12], ar[y - 12])
            if y == 12:
                slab = slab + across(sl[8], part[8], sr[8])
        slab = jnp.concatenate([slab, jnp.zeros((16, 128), F32)], axis=0)
        slab = pltpu.roll(slab, 4, 0)
        at = gy * 8 + (y - 4)
        inside = z_inside & ((at >= 0) & (at < ny * 8))
        dens[y] = jnp.where(inside, slab, 0.0).astype(BF)

    def spread_bias(ref, times):
        return jnp.concatenate([jnp.broadcast_to(ref[...], (16, 128))] * times, axis=0)

    bias1, bias2 = spread_bias(b1, 8), spread_bias(b2, 4)

    row1 = iota((128, 128), 0)

    def conv1(by, carry):
        right = jnp.concatenate(
            [
                jnp.concatenate([dens[2 * by + y, 16 * j : 16 * j + 32, :] for y in range(4)], axis=0)
                for j in range(4)
            ],
            axis=1,
        )
        out = dot(t1[...], right)
        yy = gy * 8 + 2 * by - 3 + (row1 >> 6)
        y_in = (yy >= 0) & (yy < ny * 8)
        for j in range(4):
            pre = along_x(out, 128, j) + bias1
            sig = jax.nn.sigmoid(pre)
            zz = gz * 8 + 4 * j - 4 + ((row1 >> 4) & 3)
            inside = y_in & (zz >= 0) & (zz < nz * 8)
            value = jnp.where(inside, pre * sig, 0.0).astype(BF)
            act[pl.ds(2 * by, 2), 4 * j : 4 * j + 4] = value.reshape(2, 4, 16, 128)
            slope = jnp.where(inside, sig * (1.0 + pre * (1.0 - sig)), 0.0)
            ds1[pl.ds(2 * by, 2), 4 * j : 4 * j + 4] = slope.reshape(2, 4, 16, 128)
        return carry

    lax.fori_loop(0, 7, conv1, 0)

    def block(ref, y0, z0):
        return jnp.concatenate([ref[y0 + y, z0 : z0 + 4].reshape(64, 128) for y in range(4)], axis=0)

    row2 = iota((64, 128), 0)

    def conv2(by, carry):
        right = jnp.concatenate([block(act, 2 * by, 2 * bz + 1) for bz in range(6)], axis=1)
        out = dot(t2[...], right)
        yy = gy * 8 + 2 * by - 2 + (row2 >> 5)
        y_in = (yy >= 0) & (yy < ny * 8)
        for bz in range(6):
            pre = along_x(out, 64, bz) + bias2
            sig = jax.nn.sigmoid(pre)
            zz = gz * 8 + 2 * bz - 2 + ((row2 >> 4) & 1)
            inside = y_in & (zz >= 0) & (zz < nz * 8)
            if 1 <= bz <= 4:

                @pl.when((by >= 1) & (by <= 4))
                def _():
                    refined[pl.ds(2 * by - 2, 2), 2 * bz - 2 : 2 * bz] = (
                        (pre * sig).astype(BF).reshape(2, 2, 16, 128)
                    )

            cot = cext[pl.ds(2 * by, 2), 2 * bz : 2 * bz + 2].reshape(64, 128).astype(F32)
            delta = jnp.where(inside, cot * (sig * (1.0 + pre * (1.0 - sig))), 0.0)
            d2[pl.ds(2 * by, 2), 2 * bz : 2 * bz + 2] = delta.astype(BF).reshape(2, 2, 16, 128)
        return carry

    lax.fori_loop(0, 6, conv2, 0)

    def conv3(by, carry):
        right = jnp.concatenate([block(d2, 2 * by, 2 * bz) for bz in range(5)], axis=1)
        out = dot(t2f[...], right)
        for bz in range(5):
            slope = ds1[pl.ds(2 * by + 2, 2), 2 * bz + 3 : 2 * bz + 5].reshape(64, 128)
            delta = along_x(out, 64, bz) * slope
            d1[pl.ds(2 * by, 2), 2 * bz : 2 * bz + 2] = delta.astype(BF).reshape(2, 2, 16, 128)
        return carry

    lax.fori_loop(0, 5, conv3, 0)

    g2[...] = jnp.zeros_like(g2)
    g1[...] = jnp.zeros_like(g1)
    s2[...] = jnp.zeros_like(s2)
    s1[...] = jnp.zeros_like(s1)
    table4 = t1f[...].astype(BF)

    def last(by, carry):
        right = jnp.concatenate([block(d1, 2 * by, 2 * bz) for bz in range(4)], axis=1)
        out = dot(table4, right)
        for bz in range(4):
            field[pl.ds(2 * by, 2), 2 * bz : 2 * bz + 2] = along_x(out, 32, bz).reshape(2, 2, 8, 128)

        lefts, rights = [], []
        for bz in range(4):
            delta = d2[pl.ds(2 * by + 2, 2), 2 * bz + 2 : 2 * bz + 4].reshape(64, 128).astype(F32)
            s2[...] += delta[0:16] + delta[16:32] + delta[32:48] + delta[48:64]
            lefts.append(
                jnp.concatenate([from_right(delta), delta, from_left(delta)], axis=0).astype(BF)
            )
            rights.append(block(act, 2 * by + 2, 2 * bz + 3))
        g2[...] += dot(jnp.concatenate(lefts, axis=1), jnp.concatenate(rights, axis=1), NT)

        lefts, rights = [], []
        for j in range(2):
            delta = d1[pl.ds(2 * by + 1, 2), 4 * j + 1 : 4 * j + 5].reshape(128, 128).astype(F32)
            total = delta[0:16]
            for i in range(1, 8):
                total = total + delta[16 * i : 16 * i + 16]
            s1[...] += total
            lefts.append(
                jnp.concatenate([from_right(delta), delta, from_left(delta)], axis=0).astype(BF)
            )
            rights.append(
                jnp.concatenate(
                    [dens[2 * by + 3 + y, 16 * j + 16 : 16 * j + 48, :] for y in range(4)], axis=0
                )
            )
        g1[...] += dot(jnp.concatenate(lefts, axis=1), jnp.concatenate(rights, axis=1), NT)
        return carry

    lax.fori_loop(0, 4, last, 0)

    lane16 = iota((16, 128), 1)
    for x in range(3):
        total = g2[x * 64 : x * 64 + 16]
        for i in range(1, 4):
            shift = ((i >> 1) * 4 + (i & 1)) * 16
            total = total + pltpu.roll(g2[x * 64 + 16 * i : x * 64 + 16 * i + 16], 256 - shift, 1)
        sums[16 * x : 16 * x + 16, 0:256] = total
        total = g1[x * 128 : x * 128 + 16]
        for i in range(1, 8):
            shift = (i >> 2) * 32 + (i & 3) * 4
            total = total + pltpu.roll(g1[x * 128 + 16 * i : x * 128 + 16 * i + 16], 128 - shift, 1)
        if x == 0:
            total = jnp.where(lane16 == 96, jnp.sum(s1[...], axis=1, keepdims=True), total)
            total = jnp.where(lane16 == 97, jnp.sum(s2[...], axis=1, keepdims=True), total)
        sums[16 * x : 16 * x + 16, 256:384] = total


def unet(ny, nz, *args):
    return pl.pallas_call(
        functools.partial(unet_body, ny, nz),
        out_shape=[
            jax.ShapeDtypeStruct((8, 8, 16, 128), BF),
            jax.ShapeDtypeStruct((8, 8, 8, 128), F32),
            jax.ShapeDtypeStruct((48, 384), F32),
        ],
        in_specs=[SMEM] + [VMEM] * 16,
        out_specs=[VMEM] * 3,
        scratch_shapes=[
            pltpu.VMEM((16, 80, 128), BF),
            pltpu.VMEM((14, 16, 16, 128), BF),
            pltpu.VMEM((14, 16, 16, 128), F32),
            pltpu.VMEM((12, 12, 16, 128), BF),
            pltpu.VMEM((10, 10, 16, 128), BF),
            pltpu.VMEM((192, 256), F32),
            pltpu.VMEM((384, 128), F32),
            pltpu.VMEM((16, 128), F32),
            pltpu.VMEM((16, 128), F32),
        ],
        compiler_params=pltpu.CompilerParams(vmem_limit_bytes=LIMIT),
        name="unet",
    )(*args)


def local(off, mass, vel, dest, w1, b1, w2, b2, cot):
    ny, nz = lax.axis_size("gy"), lax.axis_size("gz")
    devices = ny * nz
    count = mass.shape[0]
    slots = 2 * count // devices
    t1, t2, t2f, t1f = tables(
        w1.transpose(2, 3, 4, 1, 0).reshape(27, 4, 16), w2.transpose(2, 3, 4, 0, 1).reshape(27, 16, 16)
    )
    sent = pack(off, mass.reshape(1, count), vel, dest.reshape(1, count), devices, slots)
    got = lax.all_to_all(sent, ("gy", "gz"), split_axis=0, concat_axis=0, tiled=True)
    part = deposit(got)
    *pieces, cext = halo(part, cot.transpose(1, 2, 0, 3), ny, nz)
    pos = jnp.stack([lax.axis_index("gy"), lax.axis_index("gz")]).astype(jnp.int32)
    refined, field, sums = unet(
        ny, nz, pos, part, *pieces, cext, t1, t2, t2f, t1f, b1.reshape(16, 1), b2.reshape(16, 1)
    )
    scale = 1.0 / math.sqrt(8 * 8 * 128 * devices)
    total = lax.psum(sums, ("gy", "gz")) * scale
    second = total[:, :256].reshape(3, 16, 4, 4, 16)[:, :, :3, :3]
    first = total[:, 256:].reshape(3, 16, 4, 8, 4)[:, :, :3, :3]
    return (
        refined.transpose(2, 0, 1, 3),
        field[:, :, :4].transpose(2, 0, 1, 3),
        first.transpose(1, 4, 2, 3, 0),
        total[:16, 256 + 96],
        second.transpose(1, 4, 2, 3, 0),
        total[:16, 256 + 97],
    )


def solution(mesh):
    placed = (
        P(None, ("gy", "gz")),
        P(("gy", "gz")),
        P(None, ("gy", "gz")),
        P(("gy", "gz"), None),
        P(),
        P(),
        P(),
        P(),
        P(None, "gy", "gz", None),
    )
    return jax.shard_map(
        local,
        mesh=mesh,
        in_specs=placed,
        out_specs=(P(None, "gy", "gz", None), P(None, "gy", "gz", None), P(), P(), P(), P()),
        check_vma=False,
    )
```

```python
import functools
import math

import jax
import jax.numpy as jnp
from jax import lax
from jax.experimental import pallas as pl
from jax.experimental.pallas import tpu as pltpu
from jax.sharding import PartitionSpec as P

F32 = jnp.float32
BF = jnp.bfloat16
MESH = pl.DeviceIdType.MESH
NT = (((1,), (1,)), ((), ()))
TN = (((0,), (0,)), ((), ()))
NN = (((1,), (0,)), ((), ()))
VMEM = pl.BlockSpec(memory_space=pltpu.VMEM)
SMEM = pl.BlockSpec(memory_space=pltpu.SMEM)
LIMIT = 62 * 1024 * 1024


def dot(a, b, dims=NN):
    return lax.dot_general(a, b, dims, preferred_element_type=F32)


def iota(shape, dim):
    return lax.broadcasted_iota(jnp.int32, shape, dim)


def halves(value):
    high = value.astype(BF)
    return high, (value - high.astype(F32)).astype(BF)


def pack_body(chunk, off, mass, vel, dest, out, acc):
    blocks, _, slots = out.shape
    count = off.shape[1]
    rows = iota((blocks, chunk), 0)
    ranks = iota((slots, chunk), 0).astype(F32)
    before = (iota((chunk, chunk), 0) < iota((chunk, chunk), 1)).astype(F32).astype(BF)
    acc[...] = jnp.zeros_like(acc)

    def step(k, base):
        here = pl.ds(pl.multiple_of(k * chunk, chunk), chunk)
        hot = (rows == dest[:, here]).astype(F32)
        hot16 = hot.astype(BF)
        earlier = dot(hot16, before) + base
        rank = jnp.sum(hot * earlier, axis=0, keepdims=True)
        place = (ranks == rank).astype(F32).astype(BF)
        spot = off[:, here]
        m = mass[:, here]
        v = vel[:, here]
        planes = (
            halves(spot[2:3] * 128.0)
            + halves(spot[0:1] * 8.0)
            + halves(spot[1:2] * 8.0)
            + (m.astype(BF), (m * v[0:1]).astype(BF), (m * v[1:2]).astype(BF), (m * v[2:3]).astype(BF))
        )
        spread = jnp.concatenate([place * plane for plane in planes], axis=0)
        acc[...] += dot(hot16, spread, NT)
        return base + jnp.sum(hot, axis=1, keepdims=True)

    lax.fori_loop(0, count // chunk, step, jnp.zeros((blocks, 1), F32))

    def plane(i):
        return acc[:, i * slots : (i + 1) * slots]

    for i in range(3):
        out[:, i, :] = plane(2 * i) + plane(2 * i + 1)
    out[:, 3, :] = jnp.zeros((blocks, slots), F32)
    for i in range(4):
        out[:, 4 + i, :] = plane(6 + i)


def pack(off, mass, vel, dest, blocks, slots):
    return pl.pallas_call(
        functools.partial(pack_body, 512),
        out_shape=jax.ShapeDtypeStruct((blocks, 8, slots), F32),
        in_specs=[VMEM] * 4,
        out_specs=VMEM,
        scratch_shapes=[pltpu.VMEM((blocks, 10 * slots), F32)],
        compiler_params=pltpu.CompilerParams(vmem_limit_bytes=LIMIT),
        name="pack",
    )(off, mass, vel, dest)


GROUP = 4


def hat(grid, at):
    return jnp.maximum(1.0 - jnp.abs(grid - at), 0.0)


def deposit_body(got, out, acc):
    sources = got.shape[0]
    xs = iota((128, 128), 0).astype(F32)
    zs = (iota((40, 128), 0) >> 2).astype(F32)
    ys = iota((16, 128), 0).astype(F32)
    upper = iota((8, 128), 0) >= 4
    acc[...] = jnp.zeros_like(acc)

    def factors(s):
        t = got[s]
        wx = hat(xs, t[0:1]).astype(BF)
        q = jnp.where(upper, t, pltpu.roll(t, 4, 0))
        wzq = hat(zs, t[2:3]) * jnp.concatenate([q] * 5, axis=0)
        wy = hat(ys, t[1:2])
        return wx, jnp.concatenate([wzq * wy[y : y + 1] for y in range(9)], axis=0).astype(BF)

    def step(k, carry):
        pairs = [factors(k * GROUP + i) for i in range(GROUP)]
        right = jnp.concatenate([p[0] for p in pairs], axis=1)
        left = jnp.concatenate([p[1] for p in pairs], axis=1)
        acc[...] += dot(left, right, NT)
        return carry

    lax.fori_loop(0, sources // GROUP, step, 0)
    for y in range(9):
        out[y] = acc[y * 40 : (y + 1) * 40]


def deposit(got):
    return pl.pallas_call(
        deposit_body,
        out_shape=jax.ShapeDtypeStruct((9, 40, 128), F32),
        in_specs=[VMEM],
        out_specs=VMEM,
        scratch_shapes=[pltpu.VMEM((360, 128), F32)],
        compiler_params=pltpu.CompilerParams(vmem_limit_bytes=LIMIT),
        name="deposit",
    )(got)


Y_PART = {1: (4, 5), 0: (0, 9), -1: (0, 4)}
Z_PART = {1: (16, 24), 0: (0, 40), -1: (0, 16)}
AROUND = [(a, b) for a in (1, 0, -1) for b in (1, 0, -1) if (a, b) != (0, 0)]
C_FROM = {1: (6, 2), 0: (0, 8), -1: (0, 2)}
C_INTO = {1: 0, 0: 2, -1: 10}


def halo_body(ny, nz, part, cot, *rest):
    got, cext = rest[:8], rest[8]
    send, receive, own = rest[9:]
    me_y, me_z = lax.axis_index("gy"), lax.axis_index("gz")
    barrier = pltpu.get_barrier_semaphore()

    def device(a, b):
        return (lax.rem(me_y + a + ny, ny), lax.rem(me_z + b + nz, nz))

    for a, b in AROUND:
        pl.semaphore_signal(barrier, inc=1, device_id=device(a, b), device_id_type=MESH)
    mine = pltpu.make_async_copy(cot, cext.at[pl.ds(2, 8), pl.ds(2, 8)], own)
    mine.start()
    pl.semaphore_wait(barrier, 8)
    copies = []
    for i, (a, b) in enumerate(AROUND):
        copies.append(
            pltpu.make_async_remote_copy(
                src_ref=part.at[pl.ds(*Y_PART[a]), pl.ds(*Z_PART[b])],
                dst_ref=got[i],
                send_sem=send.at[i],
                recv_sem=receive.at[i],
                device_id=device(a, b),
                device_id_type=MESH,
            )
        )
        copies.append(
            pltpu.make_async_remote_copy(
                src_ref=cot.at[pl.ds(*C_FROM[a]), pl.ds(*C_FROM[b])],
                dst_ref=cext.at[pl.ds(C_INTO[a], C_FROM[a][1]), pl.ds(C_INTO[b], C_FROM[b][1])],
                send_sem=send.at[8 + i],
                recv_sem=receive.at[8 + i],
                device_id=device(a, b),
                device_id_type=MESH,
            )
        )
    for c in copies:
        c.start()
    mine.wait()
    for c in copies:
        c.wait()


def halo(part, cot, ny, nz):
    return pl.pallas_call(
        functools.partial(halo_body, ny, nz),
        out_shape=[jax.ShapeDtypeStruct((Y_PART[a][1], Z_PART[b][1], 128), F32) for a, b in AROUND]
        + [jax.ShapeDtypeStruct((12, 12, 16, 128), BF)],
        in_specs=[VMEM] * 2,
        out_specs=[VMEM] * 9,
        scratch_shapes=[
            pltpu.SemaphoreType.DMA((16,)),
            pltpu.SemaphoreType.DMA((16,)),
            pltpu.SemaphoreType.DMA,
        ],
        compiler_params=pltpu.CompilerParams(collective_id=1, has_side_effects=True),
        name="halo",
    )(part, cot)


def tables_body(w1, w2, t1, t2, t2f, t1f):
    lane256, lane128 = iota((16, 256), 1), iota((16, 128), 1)
    rep16 = ((lane256 & 15) == iota((16, 256), 0)).astype(F32).astype(BF)
    rep4 = ((iota((4, 128), 1) & 3) == iota((4, 128), 0)).astype(F32).astype(BF)
    lane8 = iota((8, 256), 1)

    def tap(y, z, x):
        return (y * 3 + z) * 3 + x

    def back(y, z, x):
        return tap(2 - y, 2 - z, 2 - x)

    taps = [(y, z) for y in range(3) for z in range(3)]
    for x in range(3):
        r2 = {(y, z): dot(w2[tap(y, z, x)], rep16) for y, z in taps}
        r2f = {(y, z): dot(w2[back(y, z, x)], rep16, TN) for y, z in taps}
        r1 = {(y, z): dot(w1[tap(y, z, x)], rep4, TN) for y, z in taps}
        r1f = {
            (y, z): jnp.concatenate([dot(w1[back(y, z, x)], rep16), jnp.zeros((4, 256), F32)], axis=0)
            for y, z in taps
        }
        for oy in range(2):
            for oz in range(2):
                a = jnp.zeros((16, 256), F32)
                b = jnp.zeros((16, 256), F32)
                c = jnp.zeros((8, 256), F32)
                for y, z in taps:
                    block = (oy + y) * 4 + oz + z
                    a = jnp.where((lane256 >> 4) == block, r2[y, z], a)
                    b = jnp.where((lane256 >> 4) == block, r2f[y, z], b)
                    c = jnp.where((lane8 >> 4) == block, r1f[y, z], c)
                row = (x * 4 + oy * 2 + oz) * 16
                t2[row : row + 16] = a.astype(BF)
                t2f[row : row + 16] = b.astype(BF)
                t1f[row // 2 : row // 2 + 8] = c
            for oz in range(4):
                a = jnp.zeros((16, 128), F32)
                for y, z in taps:
                    a = jnp.where((lane128 >> 2) == (oy + y) * 8 + oz + z, r1[y, z], a)
                row = (x * 8 + oy * 4 + oz) * 16
                t1[row : row + 16] = a.astype(BF)


def tables(w1, w2):
    return pl.pallas_call(
        tables_body,
        out_shape=[
            jax.ShapeDtypeStruct((384, 128), BF),
            jax.ShapeDtypeStruct((192, 256), BF),
            jax.ShapeDtypeStruct((192, 256), BF),
            jax.ShapeDtypeStruct((96, 256), F32),
        ],
        in_specs=[VMEM] * 2,
        out_specs=[VMEM] * 4,
        compiler_params=pltpu.CompilerParams(vmem_limit_bytes=LIMIT),
        name="tables",
    )(w1, w2)


def unet_body(
    ny,
    nz,
    pos,
    part,
    bl,
    bo,
    br,
    sl,
    sr,
    al,
    ao,
    ar,
    cext,
    t1,
    t2,
    t2f,
    t1f,
    b1,
    b2,
    refined,
    field,
    sums,
    dens,
    act,
    ds1,
    d2,
    d1,
    g2,
    g1,
    s2,
    s1,
):
    gy, gz = pos[0], pos[1]
    lane = iota((128, 128), 1)
    not_first, not_last = lane > 0, lane < 127

    def from_left(v):
        return jnp.where(not_first[: v.shape[0]], pltpu.roll(v, 1, 1), 0.0)

    def from_right(v):
        return jnp.where(not_last[: v.shape[0]], pltpu.roll(v, 127, 1), 0.0)

    def along_x(v, rows, j):
        cols = slice(j * 128, (j + 1) * 128)
        return from_left(v[:rows, cols]) + v[rows : 2 * rows, cols] + from_right(v[2 * rows :, cols])

    zrow = (iota((80, 128), 0) >> 2) - 5 + gz * 8
    z_inside = (zrow >= 0) & (zrow < nz * 8)

    from_side = (gz > 0).astype(F32)
    from_below = (gy > 0).astype(F32)

    def across(left, own, right):
        return jnp.concatenate(
            [
                left[0:16],
                own[0:8] + left[16:24] * from_side,
                own[8:32],
                right[0:8] + own[32:40],
                right[8:16],
            ],
            axis=0,
        )

    for y in range(16):
        if y < 4:
            slab = across(bl[y], bo[y], br[y])
        elif y < 12:
            slab = across(sl[y - 4], part[y - 4], sr[y - 4])
            if y == 4:
                slab = slab + across(bl[4], bo[4], br[4]) * from_below
        else:
            slab = across(al[y - 12], ao[y - 12], ar[y - 12])
            if y == 12:
                slab = slab + across(sl[8], part[8], sr[8])
        slab = jnp.concatenate([slab, jnp.zeros((16, 128), F32)], axis=0)
        slab = pltpu.roll(slab, 4, 0)
        at = gy * 8 + (y - 4)
        inside = z_inside & ((at >= 0) & (at < ny * 8))
        dens[y] = jnp.where(inside, slab, 0.0).astype(BF)

    def spread_bias(ref, times):
        return jnp.concatenate([jnp.broadcast_to(ref[...], (16, 128))] * times, axis=0)

    bias1, bias2 = spread_bias(b1, 8), spread_bias(b2, 4)

    row1 = iota((128, 128), 0)

    def conv1(by, carry):
        right = jnp.concatenate(
            [
                jnp.concatenate([dens[2 * by + y, 16 * j : 16 * j + 32, :] for y in range(4)], axis=0)
                for j in range(4)
            ],
            axis=1,
        )
        out = dot(t1[...], right)
        yy = gy * 8 + 2 * by - 3 + (row1 >> 6)
        y_in = (yy >= 0) & (yy < ny * 8)
        for j in range(4):
            pre = along_x(out, 128, j) + bias1
            sig = jax.nn.sigmoid(pre)
            zz = gz * 8 + 4 * j - 4 + ((row1 >> 4) & 3)
            inside = y_in & (zz >= 0) & (zz < nz * 8)
            value = jnp.where(inside, pre * sig, 0.0).astype(BF)
            act[pl.ds(2 * by, 2), 4 * j : 4 * j + 4] = value.reshape(2, 4, 16, 128)
            slope = jnp.where(inside, sig * (1.0 + pre * (1.0 - sig)), 0.0)
            ds1[pl.ds(2 * by, 2), 4 * j : 4 * j + 4] = slope.reshape(2, 4, 16, 128)
        return carry

    lax.fori_loop(0, 7, conv1, 0)

    def block(ref, y0, z0):
        return jnp.concatenate([ref[y0 + y, z0 : z0 + 4].reshape(64, 128) for y in range(4)], axis=0)

    row2 = iota((64, 128), 0)

    def conv2(by, carry):
        right = jnp.concatenate([block(act, 2 * by, 2 * bz + 1) for bz in range(6)], axis=1)
        out = dot(t2[...], right)
        yy = gy * 8 + 2 * by - 2 + (row2 >> 5)
        y_in = (yy >= 0) & (yy < ny * 8)
        for bz in range(6):
            pre = along_x(out, 64, bz) + bias2
            sig = jax.nn.sigmoid(pre)
            zz = gz * 8 + 2 * bz - 2 + ((row2 >> 4) & 1)
            inside = y_in & (zz >= 0) & (zz < nz * 8)
            if 1 <= bz <= 4:

                @pl.when((by >= 1) & (by <= 4))
                def _():
                    refined[pl.ds(2 * by - 2, 2), 2 * bz - 2 : 2 * bz] = (
                        (pre * sig).astype(BF).reshape(2, 2, 16, 128)
                    )

            cot = cext[pl.ds(2 * by, 2), 2 * bz : 2 * bz + 2].reshape(64, 128).astype(F32)
            delta = jnp.where(inside, cot * (sig * (1.0 + pre * (1.0 - sig))), 0.0)
            d2[pl.ds(2 * by, 2), 2 * bz : 2 * bz + 2] = delta.astype(BF).reshape(2, 2, 16, 128)
        return carry

    lax.fori_loop(0, 6, conv2, 0)

    def conv3(by, carry):
        right = jnp.concatenate([block(d2, 2 * by, 2 * bz) for bz in range(5)], axis=1)
        out = dot(t2f[...], right)
        for bz in range(5):
            slope = ds1[pl.ds(2 * by + 2, 2), 2 * bz + 3 : 2 * bz + 5].reshape(64, 128)
            delta = along_x(out, 64, bz) * slope
            d1[pl.ds(2 * by, 2), 2 * bz : 2 * bz + 2] = delta.astype(BF).reshape(2, 2, 16, 128)
        return carry

    lax.fori_loop(0, 5, conv3, 0)

    g2[...] = jnp.zeros_like(g2)
    g1[...] = jnp.zeros_like(g1)
    s2[...] = jnp.zeros_like(s2)
    s1[...] = jnp.zeros_like(s1)
    table4 = t1f[...].astype(BF)

    def last(by, carry):
        right = jnp.concatenate([block(d1, 2 * by, 2 * bz) for bz in range(4)], axis=1)
        out = dot(table4, right)
        for bz in range(4):
            field[pl.ds(2 * by, 2), 2 * bz : 2 * bz + 2] = along_x(out, 32, bz).reshape(2, 2, 8, 128)

        lefts, rights = [], []
        for bz in range(4):
            delta = d2[pl.ds(2 * by + 2, 2), 2 * bz + 2 : 2 * bz + 4].reshape(64, 128).astype(F32)
            s2[...] += delta[0:16] + delta[16:32] + delta[32:48] + delta[48:64]
            lefts.append(
                jnp.concatenate([from_right(delta), delta, from_left(delta)], axis=0).astype(BF)
            )
            rights.append(block(act, 2 * by + 2, 2 * bz + 3))
        g2[...] += dot(jnp.concatenate(lefts, axis=1), jnp.concatenate(rights, axis=1), NT)

        lefts, rights = [], []
        for j in range(2):
            delta = d1[pl.ds(2 * by + 1, 2), 4 * j + 1 : 4 * j + 5].reshape(128, 128).astype(F32)
            total = delta[0:16]
            for i in range(1, 8):
                total = total + delta[16 * i : 16 * i + 16]
            s1[...] += total
            lefts.append(
                jnp.concatenate([from_right(delta), delta, from_left(delta)], axis=0).astype(BF)
            )
            rights.append(
                jnp.concatenate(
                    [dens[2 * by + 3 + y, 16 * j + 16 : 16 * j + 48, :] for y in range(4)], axis=0
                )
            )
        g1[...] += dot(jnp.concatenate(lefts, axis=1), jnp.concatenate(rights, axis=1), NT)
        return carry

    lax.fori_loop(0, 4, last, 0)

    lane16 = iota((16, 128), 1)
    for x in range(3):
        wide = g2[x * 64 : x * 64 + 16]
        for i in range(1, 4):
            shift = ((i >> 1) * 4 + (i & 1)) * 16
            wide = wide + pltpu.roll(g2[x * 64 + 16 * i : x * 64 + 16 * i + 16], 256 - shift, 1)
        slim = g1[x * 128 : x * 128 + 16]
        for i in range(1, 8):
            shift = (i >> 2) * 32 + (i & 3) * 4
            slim = slim + pltpu.roll(g1[x * 128 + 16 * i : x * 128 + 16 * i + 16], 128 - shift, 1)
        low, high = wide[:, :128], wide[:, 128:]
        free = (lane16 & 63) >= 48
        low = jnp.where(free, jnp.where(lane16 < 64, pltpu.roll(slim, 48, 1), pltpu.roll(slim, 80, 1)), low)
        high = jnp.where(free, pltpu.roll(slim, 112, 1), high)
        if x == 0:
            low = jnp.where(lane16 == 60, jnp.sum(s1[...], axis=1, keepdims=True), low)
            low = jnp.where(lane16 == 61, jnp.sum(s2[...], axis=1, keepdims=True), low)
        for half in range(2):
            sums[2 * x + half] = low[8 * half : 8 * half + 8]
            sums[6 + 2 * x + half] = high[8 * half : 8 * half + 8]
    for i in range(12, 16):
        sums[i] = jnp.zeros((8, 128), F32)


def unet(ny, nz, *args):
    return pl.pallas_call(
        functools.partial(unet_body, ny, nz),
        out_shape=[
            jax.ShapeDtypeStruct((8, 8, 16, 128), BF),
            jax.ShapeDtypeStruct((8, 8, 8, 128), F32),
            jax.ShapeDtypeStruct((16, 8, 128), F32),
        ],
        in_specs=[SMEM] + [VMEM] * 16,
        out_specs=[VMEM] * 3,
        scratch_shapes=[
            pltpu.VMEM((16, 80, 128), BF),
            pltpu.VMEM((14, 16, 16, 128), BF),
            pltpu.VMEM((14, 16, 16, 128), F32),
            pltpu.VMEM((12, 12, 16, 128), BF),
            pltpu.VMEM((10, 10, 16, 128), BF),
            pltpu.VMEM((192, 256), F32),
            pltpu.VMEM((384, 128), F32),
            pltpu.VMEM((16, 128), F32),
            pltpu.VMEM((16, 128), F32),
        ],
        compiler_params=pltpu.CompilerParams(vmem_limit_bytes=LIMIT),
        name="unet",
    )(*args)


def reduce_body(ny, nz, pay, out, from_z, from_y, send, receive):
    me_y, me_z = lax.axis_index("gy"), lax.axis_index("gz")
    barrier = pltpu.get_barrier_semaphore()

    def along_z(k):
        return (me_y, lax.rem(me_z + k, nz))

    def along_y(k):
        return (lax.rem(me_y + k, ny), me_z)

    for k in range(1, nz):
        pl.semaphore_signal(barrier, inc=1, device_id=along_z(k), device_id_type=MESH)
    for k in range(1, ny):
        pl.semaphore_signal(barrier, inc=1, device_id=along_y(k), device_id_type=MESH)
    pl.semaphore_wait(barrier, nz + ny - 2)

    def copy(src, dst, sem, to):
        return pltpu.make_async_remote_copy(
            src_ref=src,
            dst_ref=dst,
            send_sem=send.at[sem],
            recv_sem=receive.at[sem],
            device_id=to,
            device_id_type=MESH,
        )

    first = [
        copy(pay.at[lax.rem(me_z + k, nz)], from_z.at[k], k, along_z(k)) for k in range(1, nz)
    ]
    for c in first:
        c.start()
    for c in first:
        c.wait()
    total = pay[me_z]
    for k in range(1, nz):
        total = total + from_z[k]
    from_y[me_y] = total
    second = [copy(from_y.at[me_y], from_y.at[me_y], nz + k, along_y(k)) for k in range(1, ny)]
    for c in second:
        c.start()
    for c in second:
        c.wait()
    total = from_y[0]
    for k in range(1, ny):
        total = total + from_y[k]
    out[me_z] = total
    third = [copy(out.at[me_z], out.at[me_z], nz + ny + k, along_z(k)) for k in range(1, nz)]
    for c in third:
        c.start()
    for c in third:
        c.wait()


def reduce(pay, ny, nz):
    return pl.pallas_call(
        functools.partial(reduce_body, ny, nz),
        out_shape=jax.ShapeDtypeStruct((nz, 8, 128), F32),
        in_specs=[VMEM],
        out_specs=VMEM,
        scratch_shapes=[
            pltpu.VMEM((nz, 8, 128), F32),
            pltpu.VMEM((ny, 8, 128), F32),
            pltpu.SemaphoreType.DMA((2 * nz + ny,)),
            pltpu.SemaphoreType.DMA((2 * nz + ny,)),
        ],
        compiler_params=pltpu.CompilerParams(collective_id=2, has_side_effects=True),
        name="reduce",
    )(pay)


def finish_body(scale, sums, first, bias1, second, bias2):
    kinds = [jnp.concatenate([sums[2 * i], sums[2 * i + 1]], axis=0) * scale for i in range(6)]
    turned = jnp.concatenate(kinds + [jnp.zeros((32, 128), F32)], axis=0).T
    for x in range(3):
        for y in range(3):
            kind = x if y < 2 else 3 + x
            base = 64 * (y & 1)
            for z in range(3):
                t = (y * 3 + z) * 3 + x
                at = base + 16 * z
                wide = pltpu.roll(kinds[kind], 128 - at, 1) if at else kinds[kind]
                second[t] = wide[:, :16]
                rows = turned[base + 48 + 4 * z : base + 52 + 4 * z]
                rows = jnp.concatenate([rows, rows], axis=0)
                slim = pltpu.roll(rows, 128 - 16 * kind, 1) if kind else rows
                first[t] = slim[:4, :16]
    bias1[...] = turned[60:61, :16]
    bias2[...] = turned[61:62, :16]


def finish(sums, scale):
    return pl.pallas_call(
        functools.partial(finish_body, scale),
        out_shape=[
            jax.ShapeDtypeStruct((27, 4, 16), F32),
            jax.ShapeDtypeStruct((1, 16), F32),
            jax.ShapeDtypeStruct((27, 16, 16), F32),
            jax.ShapeDtypeStruct((1, 16), F32),
        ],
        in_specs=[VMEM],
        out_specs=[VMEM] * 4,
        name="finish",
    )(sums)


def local(off, mass, vel, dest, w1, b1, w2, b2, cot):
    ny, nz = lax.axis_size("gy"), lax.axis_size("gz")
    devices = ny * nz
    count = mass.shape[0]
    slots = 2 * count // devices
    t1, t2, t2f, t1f = tables(
        w1.transpose(2, 3, 4, 1, 0).reshape(27, 4, 16), w2.transpose(2, 3, 4, 0, 1).reshape(27, 16, 16)
    )
    sent = pack(off, mass.reshape(1, count), vel, dest.reshape(1, count), devices, slots)
    got = lax.all_to_all(sent, ("gy", "gz"), split_axis=0, concat_axis=0, tiled=True)
    part = deposit(got)
    *pieces, cext = halo(part, cot.transpose(1, 2, 0, 3), ny, nz)
    pos = jnp.stack([lax.axis_index("gy"), lax.axis_index("gz")]).astype(jnp.int32)
    refined, field, sums = unet(
        ny, nz, pos, part, *pieces, cext, t1, t2, t2f, t1f, b1.reshape(16, 1), b2.reshape(16, 1)
    )
    scale = 1.0 / math.sqrt(8 * 8 * 128 * devices)
    first, bias1, second, bias2 = finish(reduce(sums, ny, nz), scale)
    return (
        refined.transpose(2, 0, 1, 3),
        field[:, :, :4].transpose(2, 0, 1, 3),
        first.reshape(3, 3, 3, 4, 16).transpose(4, 3, 0, 1, 2),
        bias1.reshape(16),
        second.reshape(3, 3, 3, 16, 16).transpose(3, 4, 0, 1, 2),
        bias2.reshape(16),
    )


def solution(mesh):
    placed = (
        P(None, ("gy", "gz")),
        P(("gy", "gz")),
        P(None, ("gy", "gz")),
        P(("gy", "gz"), None),
        P(),
        P(),
        P(),
        P(),
        P(None, "gy", "gz", None),
    )
    return jax.shard_map(
        local,
        mesh=mesh,
        in_specs=placed,
        out_specs=(P(None, "gy", "gz", None), P(None, "gy", "gz", None), P(), P(), P(), P()),
        check_vma=False,
    )
```

```python
import functools
import math

import jax
import jax.numpy as jnp
from jax import lax
from jax.experimental import pallas as pl
from jax.experimental.pallas import tpu as pltpu
from jax.sharding import PartitionSpec as P

F32 = jnp.float32
BF = jnp.bfloat16
MESH = pl.DeviceIdType.MESH
NT = (((1,), (1,)), ((), ()))
TN = (((0,), (0,)), ((), ()))
NN = (((1,), (0,)), ((), ()))
VMEM = pl.BlockSpec(memory_space=pltpu.VMEM)
SMEM = pl.BlockSpec(memory_space=pltpu.SMEM)
LIMIT = 62 * 1024 * 1024


def dot(a, b, dims=NN):
    return lax.dot_general(a, b, dims, preferred_element_type=F32)


def iota(shape, dim):
    return lax.broadcasted_iota(jnp.int32, shape, dim)


def halves(value):
    high = value.astype(BF)
    return high, (value - high.astype(F32)).astype(BF)


def pack_body(chunk, off, mass, vel, dest, out, acc):
    blocks, _, slots = out.shape
    count = off.shape[1]
    rows = iota((blocks, chunk), 0)
    ranks = iota((slots, chunk), 0).astype(F32)
    before = (iota((chunk, chunk), 0) < iota((chunk, chunk), 1)).astype(F32).astype(BF)
    acc[...] = jnp.zeros_like(acc)

    def step(k, base):
        here = pl.ds(pl.multiple_of(k * chunk, chunk), chunk)
        hot = (rows == dest[:, here]).astype(F32)
        hot16 = hot.astype(BF)
        earlier = dot(hot16, before) + base
        rank = jnp.sum(hot * earlier, axis=0, keepdims=True)
        place = (ranks == rank).astype(F32).astype(BF)
        spot = off[:, here]
        m = mass[:, here]
        v = vel[:, here]
        planes = (
            halves(spot[2:3] * 128.0)
            + halves(spot[0:1] * 8.0)
            + halves(spot[1:2] * 8.0)
            + (m.astype(BF), (m * v[0:1]).astype(BF), (m * v[1:2]).astype(BF), (m * v[2:3]).astype(BF))
        )
        spread = jnp.concatenate([place * plane for plane in planes], axis=0)
        acc[...] += dot(hot16, spread, NT)
        return base + jnp.sum(hot, axis=1, keepdims=True)

    lax.fori_loop(0, count // chunk, step, jnp.zeros((blocks, 1), F32))

    def plane(i):
        return acc[:, i * slots : (i + 1) * slots]

    for i in range(3):
        out[:, i, :] = plane(2 * i) + plane(2 * i + 1)
    out[:, 3, :] = jnp.zeros((blocks, slots), F32)
    for i in range(4):
        out[:, 4 + i, :] = plane(6 + i)


GROUP = 4


def hat(grid, at):
    return jnp.maximum(1.0 - jnp.abs(grid - at), 0.0)


def deposit_body(got, acc, first_ready, ready, groups):
    size = got.shape[0] // groups
    xs = iota((128, 128), 0).astype(F32)
    zs = (iota((40, 128), 0) >> 2).astype(F32)
    ys = iota((16, 128), 0).astype(F32)
    upper = iota((8, 128), 0) >= 4
    acc[...] = jnp.zeros_like(acc)

    def factors(s):
        t = got[s]
        wx = hat(xs, t[0:1]).astype(BF)
        q = jnp.where(upper, t, pltpu.roll(t, 4, 0))
        wzq = hat(zs, t[2:3]) * jnp.concatenate([q] * 5, axis=0)
        wy = hat(ys, t[1:2])
        return wx, jnp.concatenate([wzq * wy[y : y + 1] for y in range(9)], axis=0).astype(BF)

    def add(g):
        for k in range(size // GROUP):
            pairs = [factors(g * size + k * GROUP + i) for i in range(GROUP)]
            right = jnp.concatenate([p[0] for p in pairs], axis=1)
            left = jnp.concatenate([p[1] for p in pairs], axis=1)
            acc[...] += dot(left, right, NT)

    def step(g, carry):
        ready(g)
        add(g)
        return carry

    first_ready()
    add(0)
    lax.fori_loop(1, groups, step, 0)


Y_PART = {1: (4, 5), 0: (0, 9), -1: (0, 4)}
Z_PART = {1: (16, 24), 0: (0, 40), -1: (0, 16)}
AROUND = [(a, b) for a in (1, 0, -1) for b in (1, 0, -1) if (a, b) != (0, 0)]
C_FROM = {1: (6, 2), 0: (0, 8), -1: (0, 2)}
C_INTO = {1: 0, 0: 2, -1: 10}


def tables_body(w1, w2, t1, t2, t2f, t1f):
    lane256, lane128 = iota((16, 256), 1), iota((16, 128), 1)
    rep16 = ((lane256 & 15) == iota((16, 256), 0)).astype(F32).astype(BF)
    rep4 = ((iota((4, 128), 1) & 3) == iota((4, 128), 0)).astype(F32).astype(BF)
    lane8 = iota((8, 256), 1)

    def tap(y, z, x):
        return (y * 3 + z) * 3 + x

    def back(y, z, x):
        return tap(2 - y, 2 - z, 2 - x)

    taps = [(y, z) for y in range(3) for z in range(3)]
    for x in range(3):
        r2 = {(y, z): dot(w2[tap(y, z, x)], rep16) for y, z in taps}
        r2f = {(y, z): dot(w2[back(y, z, x)], rep16, TN) for y, z in taps}
        r1 = {(y, z): dot(w1[tap(y, z, x)], rep4, TN) for y, z in taps}
        r1f = {
            (y, z): jnp.concatenate([dot(w1[back(y, z, x)], rep16), jnp.zeros((4, 256), F32)], axis=0)
            for y, z in taps
        }
        for oy in range(2):
            for oz in range(2):
                a = jnp.zeros((16, 256), F32)
                b = jnp.zeros((16, 256), F32)
                c = jnp.zeros((8, 256), F32)
                for y, z in taps:
                    block = (oy + y) * 4 + oz + z
                    a = jnp.where((lane256 >> 4) == block, r2[y, z], a)
                    b = jnp.where((lane256 >> 4) == block, r2f[y, z], b)
                    c = jnp.where((lane8 >> 4) == block, r1f[y, z], c)
                row = (x * 4 + oy * 2 + oz) * 16
                t2[row : row + 16] = a.astype(BF)
                t2f[row : row + 16] = b.astype(BF)
                t1f[row // 2 : row // 2 + 8] = c
            for oz in range(4):
                a = jnp.zeros((16, 128), F32)
                for y, z in taps:
                    a = jnp.where((lane128 >> 2) == (oy + y) * 8 + oz + z, r1[y, z], a)
                row = (x * 8 + oy * 4 + oz) * 16
                t1[row : row + 16] = a.astype(BF)


def unet_body(
    ny,
    nz,
    gy,
    gz,
    part,
    bl,
    bo,
    br,
    sl,
    sr,
    al,
    ao,
    ar,
    cext,
    t1,
    t2,
    t2f,
    t1f,
    b1,
    b2,
    refined,
    field,
    sums,
    dens,
    act,
    ds1,
    d2,
    d1,
    g2,
    g1,
    s2,
    s1,
):
    lane = iota((128, 128), 1)
    not_first, not_last = lane > 0, lane < 127

    def from_left(v):
        return jnp.where(not_first[: v.shape[0]], pltpu.roll(v, 1, 1), 0.0)

    def from_right(v):
        return jnp.where(not_last[: v.shape[0]], pltpu.roll(v, 127, 1), 0.0)

    def along_x(v, rows, j):
        cols = slice(j * 128, (j + 1) * 128)
        return from_left(v[:rows, cols]) + v[rows : 2 * rows, cols] + from_right(v[2 * rows :, cols])

    zrow = (iota((80, 128), 0) >> 2) - 5 + gz * 8
    z_inside = (zrow >= 0) & (zrow < nz * 8)

    from_side = (gz > 0).astype(F32)
    from_below = (gy > 0).astype(F32)

    def across(left, own, right):
        left, own, right = left.astype(F32), own.astype(F32), right.astype(F32)
        return jnp.concatenate(
            [
                left[0:16],
                own[0:8] + left[16:24] * from_side,
                own[8:32],
                right[0:8] + own[32:40],
                right[8:16],
            ],
            axis=0,
        )

    for y in range(16):
        if y < 4:
            slab = across(bl[y], bo[y], br[y])
        elif y < 12:
            slab = across(sl[y - 4], part[(y - 4) * 40 : (y - 3) * 40], sr[y - 4])
            if y == 4:
                slab = slab + across(bl[4], bo[4], br[4]) * from_below
        else:
            slab = across(al[y - 12], ao[y - 12], ar[y - 12])
            if y == 12:
                slab = slab + across(sl[8], part[320:360], sr[8])
        slab = jnp.concatenate([slab, jnp.zeros((16, 128), F32)], axis=0)
        slab = pltpu.roll(slab, 4, 0)
        at = gy * 8 + (y - 4)
        inside = z_inside & ((at >= 0) & (at < ny * 8))
        dens[y] = jnp.where(inside, slab, 0.0).astype(BF)

    def spread_bias(ref, times):
        return jnp.concatenate([jnp.broadcast_to(ref[...], (16, 128))] * times, axis=0)

    bias1, bias2 = spread_bias(b1, 8), spread_bias(b2, 4)

    row1 = iota((128, 128), 0)

    def conv1(by, carry):
        right = jnp.concatenate(
            [
                jnp.concatenate([dens[2 * by + y, 16 * j : 16 * j + 32, :] for y in range(4)], axis=0)
                for j in range(4)
            ],
            axis=1,
        )
        out = dot(t1[...], right)
        yy = gy * 8 + 2 * by - 3 + (row1 >> 6)
        y_in = (yy >= 0) & (yy < ny * 8)
        for j in range(4):
            pre = along_x(out, 128, j) + bias1
            sig = jax.nn.sigmoid(pre)
            zz = gz * 8 + 4 * j - 4 + ((row1 >> 4) & 3)
            inside = y_in & (zz >= 0) & (zz < nz * 8)
            value = jnp.where(inside, pre * sig, 0.0).astype(BF)
            act[pl.ds(2 * by, 2), 4 * j : 4 * j + 4] = value.reshape(2, 4, 16, 128)
            slope = jnp.where(inside, sig * (1.0 + pre * (1.0 - sig)), 0.0)
            ds1[pl.ds(2 * by, 2), 4 * j : 4 * j + 4] = slope.reshape(2, 4, 16, 128)
        return carry

    lax.fori_loop(0, 7, conv1, 0)

    def block(ref, y0, z0):
        return jnp.concatenate([ref[y0 + y, z0 : z0 + 4].reshape(64, 128) for y in range(4)], axis=0)

    row2 = iota((64, 128), 0)

    def conv2(by, carry):
        right = jnp.concatenate([block(act, 2 * by, 2 * bz + 1) for bz in range(6)], axis=1)
        out = dot(t2[...], right)
        yy = gy * 8 + 2 * by - 2 + (row2 >> 5)
        y_in = (yy >= 0) & (yy < ny * 8)
        for bz in range(6):
            pre = along_x(out, 64, bz) + bias2
            sig = jax.nn.sigmoid(pre)
            zz = gz * 8 + 2 * bz - 2 + ((row2 >> 4) & 1)
            inside = y_in & (zz >= 0) & (zz < nz * 8)
            if 1 <= bz <= 4:

                @pl.when((by >= 1) & (by <= 4))
                def _():
                    refined[pl.ds(2 * by - 2, 2), 2 * bz - 2 : 2 * bz] = (
                        (pre * sig).astype(BF).reshape(2, 2, 16, 128)
                    )

            cot = cext[pl.ds(2 * by, 2), 2 * bz : 2 * bz + 2].reshape(64, 128).astype(F32)
            delta = jnp.where(inside, cot * (sig * (1.0 + pre * (1.0 - sig))), 0.0)
            d2[pl.ds(2 * by, 2), 2 * bz : 2 * bz + 2] = delta.astype(BF).reshape(2, 2, 16, 128)
        return carry

    lax.fori_loop(0, 6, conv2, 0)

    def conv3(by, carry):
        right = jnp.concatenate([block(d2, 2 * by, 2 * bz) for bz in range(5)], axis=1)
        out = dot(t2f[...], right)
        for bz in range(5):
            slope = ds1[pl.ds(2 * by + 2, 2), 2 * bz + 3 : 2 * bz + 5].reshape(64, 128)
            delta = along_x(out, 64, bz) * slope
            d1[pl.ds(2 * by, 2), 2 * bz : 2 * bz + 2] = delta.astype(BF).reshape(2, 2, 16, 128)
        return carry

    lax.fori_loop(0, 5, conv3, 0)

    g2[...] = jnp.zeros_like(g2)
    g1[...] = jnp.zeros_like(g1)
    s2[...] = jnp.zeros_like(s2)
    s1[...] = jnp.zeros_like(s1)
    table4 = t1f[...].astype(BF)

    def last(by, carry):
        right = jnp.concatenate([block(d1, 2 * by, 2 * bz) for bz in range(4)], axis=1)
        out = dot(table4, right)
        for bz in range(4):
            field[pl.ds(2 * by, 2), 2 * bz : 2 * bz + 2] = along_x(out, 32, bz).reshape(2, 2, 8, 128)

        lefts, rights = [], []
        for bz in range(4):
            delta = d2[pl.ds(2 * by + 2, 2), 2 * bz + 2 : 2 * bz + 4].reshape(64, 128).astype(F32)
            s2[...] += delta[0:16] + delta[16:32] + delta[32:48] + delta[48:64]
            lefts.append(
                jnp.concatenate([from_right(delta), delta, from_left(delta)], axis=0).astype(BF)
            )
            rights.append(block(act, 2 * by + 2, 2 * bz + 3))
        g2[...] += dot(jnp.concatenate(lefts, axis=1), jnp.concatenate(rights, axis=1), NT)

        lefts, rights = [], []
        for j in range(2):
            delta = d1[pl.ds(2 * by + 1, 2), 4 * j + 1 : 4 * j + 5].reshape(128, 128).astype(F32)
            total = delta[0:16]
            for i in range(1, 8):
                total = total + delta[16 * i : 16 * i + 16]
            s1[...] += total
            lefts.append(
                jnp.concatenate([from_right(delta), delta, from_left(delta)], axis=0).astype(BF)
            )
            rights.append(
                jnp.concatenate(
                    [dens[2 * by + 3 + y, 16 * j + 16 : 16 * j + 48, :] for y in range(4)], axis=0
                )
            )
        g1[...] += dot(jnp.concatenate(lefts, axis=1), jnp.concatenate(rights, axis=1), NT)
        return carry

    lax.fori_loop(0, 4, last, 0)

    lane16 = iota((16, 128), 1)
    for x in range(3):
        wide = g2[x * 64 : x * 64 + 16]
        for i in range(1, 4):
            shift = ((i >> 1) * 4 + (i & 1)) * 16
            wide = wide + pltpu.roll(g2[x * 64 + 16 * i : x * 64 + 16 * i + 16], 256 - shift, 1)
        slim = g1[x * 128 : x * 128 + 16]
        for i in range(1, 8):
            shift = (i >> 2) * 32 + (i & 3) * 4
            slim = slim + pltpu.roll(g1[x * 128 + 16 * i : x * 128 + 16 * i + 16], 128 - shift, 1)
        low, high = wide[:, :128], wide[:, 128:]
        free = (lane16 & 63) >= 48
        low = jnp.where(free, jnp.where(lane16 < 64, pltpu.roll(slim, 48, 1), pltpu.roll(slim, 80, 1)), low)
        high = jnp.where(free, pltpu.roll(slim, 112, 1), high)
        if x == 0:
            low = jnp.where(lane16 == 60, jnp.sum(s1[...], axis=1, keepdims=True), low)
            low = jnp.where(lane16 == 61, jnp.sum(s2[...], axis=1, keepdims=True), low)
        for half in range(2):
            sums[2 * x + half] = low[8 * half : 8 * half + 8]
            sums[6 + 2 * x + half] = high[8 * half : 8 * half + 8]
    for i in range(12, 16):
        sums[i] = jnp.zeros((8, 128), F32)


def reduce_body(ny, nz, me_y, me_z, pay, out, from_z, from_y, send, receive):
    def along_z(k):
        return (me_y, lax.rem(me_z + k, nz))

    def along_y(k):
        return (lax.rem(me_y + k, ny), me_z)

    def copy(src, dst, sem, to):
        return pltpu.make_async_remote_copy(
            src_ref=src,
            dst_ref=dst,
            send_sem=send.at[sem],
            recv_sem=receive.at[sem],
            device_id=to,
            device_id_type=MESH,
        )

    first = [
        copy(pay.at[lax.rem(me_z + k, nz)], from_z.at[k], k, along_z(k)) for k in range(1, nz)
    ]
    for c in first:
        c.start()
    for c in first:
        c.wait()
    total = pay[me_z]
    for k in range(1, nz):
        total = total + from_z[k]
    from_y[me_y] = total
    second = [copy(from_y.at[me_y], from_y.at[me_y], nz + k, along_y(k)) for k in range(1, ny)]
    for c in second:
        c.start()
    for c in second:
        c.wait()
    total = from_y[0]
    for k in range(1, ny):
        total = total + from_y[k]
    out[me_z] = total
    third = [copy(out.at[me_z], out.at[me_z], nz + ny + k, along_z(k)) for k in range(1, nz)]
    for c in third:
        c.start()
    for c in third:
        c.wait()


def finish_body(scale, sums, first, bias1, second, bias2):
    kinds = [jnp.concatenate([sums[2 * i], sums[2 * i + 1]], axis=0) * scale for i in range(6)]
    turned = jnp.concatenate(kinds + [jnp.zeros((32, 128), F32)], axis=0).T
    for x in range(3):
        for y in range(3):
            kind = x if y < 2 else 3 + x
            base = 64 * (y & 1)
            for z in range(3):
                t = (y * 3 + z) * 3 + x
                at = base + 16 * z
                wide = pltpu.roll(kinds[kind], 128 - at, 1) if at else kinds[kind]
                second[t] = wide[:, :16]
                rows = turned[base + 48 + 4 * z : base + 52 + 4 * z]
                rows = jnp.concatenate([rows, rows], axis=0)
                slim = pltpu.roll(rows, 128 - 16 * kind, 1) if kind else rows
                first[t] = slim[:4, :16]
    bias1[...] = turned[60:61, :16]
    bias2[...] = turned[61:62, :16]


def finish(sums, scale):
    return pl.pallas_call(
        functools.partial(finish_body, scale),
        out_shape=[
            jax.ShapeDtypeStruct((27, 4, 16), F32),
            jax.ShapeDtypeStruct((1, 16), F32),
            jax.ShapeDtypeStruct((27, 16, 16), F32),
            jax.ShapeDtypeStruct((1, 16), F32),
        ],
        in_specs=[VMEM],
        out_specs=[VMEM] * 4,
        name="finish",
    )(sums)


GROUPS = 16


def step_body(ny, nz, off, mass, vel, dest, cot, w1, w2, b1, b2, refined, field, sums, *rest):
    (sent, pile, got, part, part16, cext, t1, t2, t2f, t1f, dens, act, ds1, d2, d1, g2, g1, s2, s1) = rest[:19]
    pieces, (pay, from_z, from_y) = rest[19:27], rest[27:30]
    out_all, in_group, out_halo, in_halo, out_sum, in_sum = rest[30:]
    me_y, me_z = lax.axis_index("gy"), lax.axis_index("gz")
    devices = ny * nz
    size = devices // GROUPS
    barrier = pltpu.get_barrier_semaphore()

    def partner(j):
        k = lax.rem(j * 37, devices)
        return (lax.rem(me_y + k // nz, ny), lax.rem(me_z + lax.rem(k, nz), nz))

    def device(a, b):
        return (lax.rem(me_y + a + ny, ny), lax.rem(me_z + b + nz, nz))

    def greet(j, carry):
        pl.semaphore_signal(barrier, inc=1, device_id=partner(j), device_id_type=MESH)
        return carry

    lax.fori_loop(1, devices, greet, 0)

    cext[2:10, 2:10] = cot[...]
    tables_body(w1, w2, t1, t2, t2f, t1f)
    pack_body(512, off, mass, vel, dest, sent, pile)

    pl.semaphore_wait(barrier, devices - 1)

    def send(j, carry):
        y, z = partner(j)
        pltpu.make_async_remote_copy(
            src_ref=sent.at[y * nz + z],
            dst_ref=got.at[j],
            send_sem=out_all,
            recv_sem=in_group.at[j // size],
            device_id=(y, z),
            device_id_type=MESH,
        ).start()
        return carry

    lax.fori_loop(1, devices, send, 0)
    got[0] = sent[me_y * nz + me_z]

    def halo(i, src, dst):
        copy = pltpu.make_async_remote_copy(
            src_ref=src,
            dst_ref=dst,
            send_sem=out_halo.at[i],
            recv_sem=in_halo.at[i],
            device_id=device(*AROUND[i % 8]),
            device_id_type=MESH,
        )
        copy.start()
        return copy

    copies = [
        halo(
            8 + i,
            cot.at[pl.ds(*C_FROM[a]), pl.ds(*C_FROM[b])],
            cext.at[pl.ds(C_INTO[a], C_FROM[a][1]), pl.ds(C_INTO[b], C_FROM[b][1])],
        )
        for i, (a, b) in enumerate(AROUND)
    ]

    def landed(first, count, g):
        pltpu.make_async_remote_copy(
            src_ref=sent.at[pl.ds(0, count)],
            dst_ref=got.at[pl.ds(first, count)],
            send_sem=out_all,
            recv_sem=in_group.at[g],
            device_id=device(0, 1),
            device_id_type=MESH,
        ).wait_recv()

    deposit_body(got, part, lambda: landed(1, size - 1, 0), lambda g: landed(g * size, size, g), GROUPS)
    for y in range(9):
        part16[y] = part[y * 40 : (y + 1) * 40].astype(BF)
    copies += [
        halo(i, part16.at[pl.ds(*Y_PART[a]), pl.ds(*Z_PART[b])], pieces[i]) for i, (a, b) in enumerate(AROUND)
    ]
    pltpu.make_async_remote_copy(
        src_ref=sent.at[pl.ds(1, devices - 1)],
        dst_ref=got.at[pl.ds(1, devices - 1)],
        send_sem=out_all,
        recv_sem=in_group.at[0],
        device_id=device(0, 1),
        device_id_type=MESH,
    ).wait_send()
    for c in copies:
        c.wait()

    unet_body(
        ny, nz, me_y, me_z, part, *pieces, cext, t1, t2, t2f, t1f, b1, b2,
        refined, field, pay, dens, act, ds1, d2, d1, g2, g1, s2, s1,
    )
    reduce_body(ny, nz, me_y, me_z, pay, sums, from_z, from_y, out_sum, in_sum)


def whole_step(ny, nz, slots, *args):
    devices = ny * nz
    return pl.pallas_call(
        functools.partial(step_body, ny, nz),
        out_shape=[
            jax.ShapeDtypeStruct((8, 8, 16, 128), BF),
            jax.ShapeDtypeStruct((8, 8, 8, 128), F32),
            jax.ShapeDtypeStruct((nz, 8, 128), F32),
        ],
        in_specs=[VMEM] * 9,
        out_specs=[VMEM] * 3,
        scratch_shapes=[
            pltpu.VMEM((devices, 8, slots), F32),
            pltpu.VMEM((devices, 10 * slots), F32),
            pltpu.VMEM((devices, 8, slots), F32),
            pltpu.VMEM((360, 128), F32),
            pltpu.VMEM((9, 40, 128), BF),
            pltpu.VMEM((12, 12, 16, 128), BF),
            pltpu.VMEM((384, 128), BF),
            pltpu.VMEM((192, 256), BF),
            pltpu.VMEM((192, 256), BF),
            pltpu.VMEM((96, 256), F32),
            pltpu.VMEM((16, 80, 128), BF),
            pltpu.VMEM((14, 16, 16, 128), BF),
            pltpu.VMEM((14, 16, 16, 128), F32),
            pltpu.VMEM((12, 12, 16, 128), BF),
            pltpu.VMEM((10, 10, 16, 128), BF),
            pltpu.VMEM((192, 256), F32),
            pltpu.VMEM((384, 128), F32),
            pltpu.VMEM((16, 128), F32),
            pltpu.VMEM((16, 128), F32),
        ]
        + [pltpu.VMEM((Y_PART[a][1], Z_PART[b][1], 128), BF) for a, b in AROUND]
        + [
            pltpu.VMEM((nz, 8, 128), F32),
            pltpu.VMEM((nz, 8, 128), F32),
            pltpu.VMEM((ny, 8, 128), F32),
            pltpu.SemaphoreType.DMA,
            pltpu.SemaphoreType.DMA((GROUPS,)),
            pltpu.SemaphoreType.DMA((16,)),
            pltpu.SemaphoreType.DMA((16,)),
            pltpu.SemaphoreType.DMA((2 * nz + ny,)),
            pltpu.SemaphoreType.DMA((2 * nz + ny,)),
        ],
        compiler_params=pltpu.CompilerParams(collective_id=1, has_side_effects=True, vmem_limit_bytes=LIMIT),
        name="step",
    )(*args)


def local(off, mass, vel, dest, w1, b1, w2, b2, cot):
    ny, nz = lax.axis_size("gy"), lax.axis_size("gz")
    devices = ny * nz
    count = mass.shape[0]
    scale = 1.0 / math.sqrt(8 * 8 * 128 * devices)
    refined, field, sums = whole_step(
        ny,
        nz,
        2 * count // devices,
        off,
        mass.reshape(1, count),
        vel,
        dest.reshape(1, count),
        cot.transpose(1, 2, 0, 3),
        w1.transpose(2, 3, 4, 1, 0).reshape(27, 4, 16),
        w2.transpose(2, 3, 4, 0, 1).reshape(27, 16, 16),
        b1.reshape(16, 1),
        b2.reshape(16, 1),
    )
    first, bias1, second, bias2 = finish(sums, scale)
    return (
        refined.transpose(2, 0, 1, 3),
        field[:, :, :4].transpose(2, 0, 1, 3),
        first.reshape(3, 3, 3, 4, 16).transpose(4, 3, 0, 1, 2),
        bias1.reshape(16),
        second.reshape(3, 3, 3, 16, 16).transpose(3, 4, 0, 1, 2),
        bias2.reshape(16),
    )


def solution(mesh):
    placed = (
        P(None, ("gy", "gz")),
        P(("gy", "gz")),
        P(None, ("gy", "gz")),
        P(("gy", "gz"), None),
        P(),
        P(),
        P(),
        P(),
        P(None, "gy", "gz", None),
    )
    return jax.shard_map(
        local,
        mesh=mesh,
        in_specs=placed,
        out_specs=(P(None, "gy", "gz", None), P(None, "gy", "gz", None), P(), P(), P(), P()),
        check_vma=False,
    )
```

```python
import functools
import math

import jax
import jax.numpy as jnp
from jax import lax
from jax.experimental import pallas as pl
from jax.experimental.pallas import tpu as pltpu
from jax.sharding import PartitionSpec as P

F32 = jnp.float32
BF = jnp.bfloat16
MESH = pl.DeviceIdType.MESH
NT = (((1,), (1,)), ((), ()))
TN = (((0,), (0,)), ((), ()))
NN = (((1,), (0,)), ((), ()))
VMEM = pl.BlockSpec(memory_space=pltpu.VMEM)
SMEM = pl.BlockSpec(memory_space=pltpu.SMEM)
LIMIT = 62 * 1024 * 1024


def dot(a, b, dims=NN):
    return lax.dot_general(a, b, dims, preferred_element_type=F32)


def iota(shape, dim):
    return lax.broadcasted_iota(jnp.int32, shape, dim)


def halves(value):
    high = value.astype(BF)
    return high, (value - high.astype(F32)).astype(BF)


def rank_body(chunk, dest, codes, seats, blocks):
    count, width = dest.shape[1], 256
    rows = iota((blocks, chunk), 0)
    before = (iota((width, width), 0) < iota((width, width), 1)).astype(F32).astype(BF)

    def step(k, base):
        here = pl.ds(pl.multiple_of(k * chunk, chunk), chunk)
        to = dest[:, here]
        hot = (rows == to).astype(F32)
        hot16 = hot.astype(BF)
        ranks = []
        for i in range(chunk // width):
            cols = slice(i * width, (i + 1) * width)
            earlier = dot(hot16[:, cols], before) + base
            ranks.append(jnp.sum(hot[:, cols] * earlier, axis=0, keepdims=True))
            base = base + jnp.sum(hot[:, cols], axis=1, keepdims=True)
        rank = jnp.concatenate(ranks, axis=1).astype(jnp.int32)
        codes[:, here] = to + (rank & 1) * blocks
        seats[:, here] = rank >> 1
        return base

    lax.fori_loop(0, count // chunk, step, jnp.zeros((blocks, 1), F32))


def pack_body(chunk, off, mass, vel, codes, seats, out, acc):
    blocks, _, slots = out.shape
    count, half = off.shape[1], slots // 2
    rows = iota((2 * blocks, chunk), 0).astype(F32).astype(BF)
    ranks = iota((half, chunk), 0).astype(F32).astype(BF)
    one, zero = jnp.ones((), BF), jnp.zeros((), BF)
    acc[...] = jnp.zeros_like(acc)

    def step(k, carry):
        here = pl.ds(pl.multiple_of(k * chunk, chunk), chunk)
        hot = jnp.where(rows == codes[:, here].astype(F32).astype(BF), one, zero)
        taken = ranks == seats[:, here].astype(F32).astype(BF)
        spot = off[:, here]
        m = mass[:, here]
        v = vel[:, here]
        planes = (
            halves(spot[2:3] * 128.0)
            + halves(spot[0:1] * 8.0)
            + halves(spot[1:2] * 8.0)
            + (m.astype(BF), (m * v[0:1]).astype(BF), (m * v[1:2]).astype(BF), (m * v[2:3]).astype(BF))
        )
        spread = jnp.concatenate([jnp.where(taken, plane, zero) for plane in planes], axis=0)
        acc[...] += dot(hot, spread, NT)
        return carry

    lax.fori_loop(0, count // chunk, step, 0)
    low_half = iota((blocks, slots), 1) < half

    def plane(i):
        cols = slice(i // 2 * slots, (i // 2 + 1) * slots)
        even, odd = acc[:blocks, cols], acc[blocks:, cols]
        if i % 2:
            return jnp.where(low_half, pltpu.roll(even, half, 1), odd)
        return jnp.where(low_half, even, pltpu.roll(odd, half, 1))

    for i in range(3):
        out[:, i, :] = plane(2 * i) + plane(2 * i + 1)
    out[:, 3, :] = jnp.zeros((blocks, slots), F32)
    for i in range(4):
        out[:, 4 + i, :] = plane(6 + i)


GROUP = 16


def hat(grid, at):
    return jnp.maximum(1.0 - jnp.abs(grid - at), 0.0)


def deposit_body(got, acc, first_ready, ready, groups):
    size = got.shape[0] // groups
    xs = iota((128, 128), 0).astype(F32)
    zs = (iota((40, 128), 0) >> 2).astype(F32)
    ys = iota((16, 128), 0).astype(F32)
    upper = iota((8, 128), 0) >= 4
    acc[...] = jnp.zeros_like(acc)

    def factors(s):
        t = got[s]
        wx = hat(xs, t[0:1]).astype(BF)
        q = jnp.where(upper, t, pltpu.roll(t, 4, 0))
        wzq = hat(zs, t[2:3]) * jnp.concatenate([q] * 5, axis=0)
        wy = hat(ys, t[1:2])
        return wx, jnp.concatenate([wzq * wy[y : y + 1] for y in range(9)], axis=0).astype(BF)

    def add(g):
        for k in range(size // GROUP):
            pairs = [factors(g * size + k * GROUP + i) for i in range(GROUP)]
            right = jnp.concatenate([p[0] for p in pairs], axis=1)
            left = jnp.concatenate([p[1] for p in pairs], axis=1)
            acc[...] += dot(left, right, NT)

    def step(g, carry):
        ready(g)
        add(g)
        return carry

    first_ready()
    add(0)
    lax.fori_loop(1, groups, step, 0)


Y_PART = {1: (4, 5), 0: (0, 9), -1: (0, 4)}
Z_PART = {1: (16, 24), 0: (0, 40), -1: (0, 16)}
AROUND = [(a, b) for a in (1, 0, -1) for b in (1, 0, -1) if (a, b) != (0, 0)]
C_FROM = {1: (6, 2), 0: (0, 8), -1: (0, 2)}
C_INTO = {1: 0, 0: 2, -1: 10}


def tables_body(w1, w2, t1, t2, t2f, t1f):
    lane256, lane128 = iota((16, 256), 1), iota((16, 128), 1)
    rep16 = ((lane256 & 15) == iota((16, 256), 0)).astype(F32).astype(BF)
    rep4 = ((iota((4, 128), 1) & 3) == iota((4, 128), 0)).astype(F32).astype(BF)
    lane8 = iota((8, 256), 1)

    def tap(y, z, x):
        return (y * 3 + z) * 3 + x

    def back(y, z, x):
        return tap(2 - y, 2 - z, 2 - x)

    taps = [(y, z) for y in range(3) for z in range(3)]
    for x in range(3):
        r2 = {(y, z): dot(w2[tap(y, z, x)], rep16) for y, z in taps}
        r2f = {(y, z): dot(w2[back(y, z, x)], rep16, TN) for y, z in taps}
        r1 = {(y, z): dot(w1[tap(y, z, x)], rep4, TN) for y, z in taps}
        r1f = {
            (y, z): jnp.concatenate([dot(w1[back(y, z, x)], rep16), jnp.zeros((4, 256), F32)], axis=0)
            for y, z in taps
        }
        for oy in range(2):
            for oz in range(2):
                a = jnp.zeros((16, 256), F32)
                b = jnp.zeros((16, 256), F32)
                c = jnp.zeros((8, 256), F32)
                for y, z in taps:
                    block = (oy + y) * 4 + oz + z
                    a = jnp.where((lane256 >> 4) == block, r2[y, z], a)
                    b = jnp.where((lane256 >> 4) == block, r2f[y, z], b)
                    c = jnp.where((lane8 >> 4) == block, r1f[y, z], c)
                row = (x * 4 + oy * 2 + oz) * 16
                t2[row : row + 16] = a.astype(BF)
                t2f[row : row + 16] = b.astype(BF)
                t1f[row // 2 : row // 2 + 8] = c
            for oz in range(4):
                a = jnp.zeros((16, 128), F32)
                for y, z in taps:
                    a = jnp.where((lane128 >> 2) == (oy + y) * 8 + oz + z, r1[y, z], a)
                row = (x * 8 + oy * 4 + oz) * 16
                t1[row : row + 16] = a.astype(BF)


def unet_body(
    ny,
    nz,
    gy,
    gz,
    part,
    bl,
    bo,
    br,
    sl,
    sr,
    al,
    ao,
    ar,
    cext,
    t1,
    t2,
    t2f,
    t1f,
    b1,
    b2,
    refined,
    field,
    sums,
    dens,
    act,
    ds1,
    d2,
    d1,
    g2,
    g1,
    s2,
    s1,
):
    lane = iota((128, 128), 1)
    not_first, not_last = lane > 0, lane < 127

    def from_left(v):
        return jnp.where(not_first[: v.shape[0]], pltpu.roll(v, 1, 1), 0.0)

    def from_right(v):
        return jnp.where(not_last[: v.shape[0]], pltpu.roll(v, 127, 1), 0.0)

    def along_x(v, rows, j):
        cols = slice(j * 128, (j + 1) * 128)
        return from_left(v[:rows, cols]) + v[rows : 2 * rows, cols] + from_right(v[2 * rows :, cols])

    zrow = (iota((80, 128), 0) >> 2) - 5 + gz * 8
    z_inside = (zrow >= 0) & (zrow < nz * 8)

    from_side = (gz > 0).astype(F32)
    from_below = (gy > 0).astype(F32)

    def across(left, own, right):
        left, own, right = left.astype(F32), own.astype(F32), right.astype(F32)
        return jnp.concatenate(
            [
                left[0:16],
                own[0:8] + left[16:24] * from_side,
                own[8:32],
                right[0:8] + own[32:40],
                right[8:16],
            ],
            axis=0,
        )

    for y in range(16):
        if y < 4:
            slab = across(bl[y], bo[y], br[y])
        elif y < 12:
            slab = across(sl[y - 4], part[(y - 4) * 40 : (y - 3) * 40], sr[y - 4])
            if y == 4:
                slab = slab + across(bl[4], bo[4], br[4]) * from_below
        else:
            slab = across(al[y - 12], ao[y - 12], ar[y - 12])
            if y == 12:
                slab = slab + across(sl[8], part[320:360], sr[8])
        slab = jnp.concatenate([slab, jnp.zeros((16, 128), F32)], axis=0)
        slab = pltpu.roll(slab, 4, 0)
        at = gy * 8 + (y - 4)
        inside = z_inside & ((at >= 0) & (at < ny * 8))
        dens[y] = jnp.where(inside, slab, 0.0).astype(BF)

    diagonal = iota((16, 16), 0) == iota((16, 16), 1)

    def spread_bias(ref, times):
        column = jnp.sum(jnp.where(diagonal, ref[...], 0.0), axis=1, keepdims=True)
        return jnp.concatenate([jnp.broadcast_to(column, (16, 128))] * times, axis=0)

    bias1, bias2 = spread_bias(b1, 8), spread_bias(b2, 4)

    row1 = iota((128, 128), 0)

    def conv1(by):
        right = jnp.concatenate(
            [
                jnp.concatenate([dens[2 * by + y, 16 * j : 16 * j + 32, :] for y in range(4)], axis=0)
                for j in range(4)
            ],
            axis=1,
        )
        out = dot(t1[...], right)
        yy = gy * 8 + 2 * by - 3 + (row1 >> 6)
        y_in = (yy >= 0) & (yy < ny * 8)
        for j in range(4):
            pre = along_x(out, 128, j) + bias1
            sig = jax.nn.sigmoid(pre)
            zz = gz * 8 + 4 * j - 4 + ((row1 >> 4) & 3)
            inside = y_in & (zz >= 0) & (zz < nz * 8)
            value = jnp.where(inside, pre * sig, 0.0).astype(BF)
            act[pl.ds(2 * by, 2), 4 * j : 4 * j + 4] = value.reshape(2, 4, 16, 128)
            slope = jnp.where(inside, sig * (1.0 + pre * (1.0 - sig)), 0.0)
            ds1[pl.ds(2 * by, 2), 4 * j : 4 * j + 4] = slope.reshape(2, 4, 16, 128)

    for by in range(7):
        conv1(by)

    def block(ref, y0, z0):
        return jnp.concatenate([ref[y0 + y, z0 : z0 + 4].reshape(64, 128) for y in range(4)], axis=0)

    row2 = iota((64, 128), 0)

    def conv2(by):
        right = jnp.concatenate([block(act, 2 * by, 2 * bz + 1) for bz in range(6)], axis=1)
        out = dot(t2[...], right)
        yy = gy * 8 + 2 * by - 2 + (row2 >> 5)
        y_in = (yy >= 0) & (yy < ny * 8)
        for bz in range(6):
            pre = along_x(out, 64, bz) + bias2
            sig = jax.nn.sigmoid(pre)
            zz = gz * 8 + 2 * bz - 2 + ((row2 >> 4) & 1)
            inside = y_in & (zz >= 0) & (zz < nz * 8)
            if 1 <= bz <= 4 and 1 <= by <= 4:
                refined[2 * by - 2 : 2 * by, 2 * bz - 2 : 2 * bz] = (pre * sig).reshape(2, 2, 16, 128)

            cot = cext[pl.ds(2 * by, 2), 2 * bz : 2 * bz + 2].reshape(64, 128).astype(F32)
            delta = jnp.where(inside, cot * (sig * (1.0 + pre * (1.0 - sig))), 0.0)
            d2[pl.ds(2 * by, 2), 2 * bz : 2 * bz + 2] = delta.astype(BF).reshape(2, 2, 16, 128)

    for by in range(6):
        conv2(by)

    def conv3(by):
        right = jnp.concatenate([block(d2, 2 * by, 2 * bz) for bz in range(5)], axis=1)
        out = dot(t2f[...], right)
        for bz in range(5):
            slope = ds1[pl.ds(2 * by + 2, 2), 2 * bz + 3 : 2 * bz + 5].reshape(64, 128)
            delta = along_x(out, 64, bz) * slope
            d1[pl.ds(2 * by, 2), 2 * bz : 2 * bz + 2] = delta.astype(BF).reshape(2, 2, 16, 128)

    for by in range(5):
        conv3(by)

    g2[...] = jnp.zeros_like(g2)
    g1[...] = jnp.zeros_like(g1)
    s2[...] = jnp.zeros_like(s2)
    s1[...] = jnp.zeros_like(s1)
    table4 = t1f[...].astype(BF)

    def last(by):
        right = jnp.concatenate([block(d1, 2 * by, 2 * bz) for bz in range(4)], axis=1)
        out = dot(table4, right)
        for bz in range(4):
            field[pl.ds(2 * by, 2), 2 * bz : 2 * bz + 2] = along_x(out, 32, bz).reshape(2, 2, 8, 128)

        lefts, rights = [], []
        for bz in range(4):
            delta = d2[pl.ds(2 * by + 2, 2), 2 * bz + 2 : 2 * bz + 4].reshape(64, 128).astype(F32)
            s2[...] += delta[0:16] + delta[16:32] + delta[32:48] + delta[48:64]
            lefts.append(
                jnp.concatenate([from_right(delta), delta, from_left(delta)], axis=0).astype(BF)
            )
            rights.append(block(act, 2 * by + 2, 2 * bz + 3))
        g2[...] += dot(jnp.concatenate(lefts, axis=1), jnp.concatenate(rights, axis=1), NT)

        lefts, rights = [], []
        for j in range(2):
            delta = d1[pl.ds(2 * by + 1, 2), 4 * j + 1 : 4 * j + 5].reshape(128, 128).astype(F32)
            total = delta[0:16]
            for i in range(1, 8):
                total = total + delta[16 * i : 16 * i + 16]
            s1[...] += total
            lefts.append(
                jnp.concatenate([from_right(delta), delta, from_left(delta)], axis=0).astype(BF)
            )
            rights.append(
                jnp.concatenate(
                    [dens[2 * by + 3 + y, 16 * j + 16 : 16 * j + 48, :] for y in range(4)], axis=0
                )
            )
        g1[...] += dot(jnp.concatenate(lefts, axis=1), jnp.concatenate(rights, axis=1), NT)

    for by in range(4):
        last(by)

    lane16 = iota((16, 128), 1)
    for x in range(3):
        wide = g2[x * 64 : x * 64 + 16]
        for i in range(1, 4):
            shift = ((i >> 1) * 4 + (i & 1)) * 16
            wide = wide + pltpu.roll(g2[x * 64 + 16 * i : x * 64 + 16 * i + 16], 256 - shift, 1)
        slim = g1[x * 128 : x * 128 + 16]
        for i in range(1, 8):
            shift = (i >> 2) * 32 + (i & 3) * 4
            slim = slim + pltpu.roll(g1[x * 128 + 16 * i : x * 128 + 16 * i + 16], 128 - shift, 1)
        low, high = wide[:, :128], wide[:, 128:]
        free = (lane16 & 63) >= 48
        low = jnp.where(free, jnp.where(lane16 < 64, pltpu.roll(slim, 48, 1), pltpu.roll(slim, 80, 1)), low)
        high = jnp.where(free, pltpu.roll(slim, 112, 1), high)
        if x == 0:
            low = jnp.where(lane16 == 60, jnp.sum(s1[...], axis=1, keepdims=True), low)
            low = jnp.where(lane16 == 61, jnp.sum(s2[...], axis=1, keepdims=True), low)
        for half in range(2):
            sums[2 * x + half] = low[8 * half : 8 * half + 8]
            sums[6 + 2 * x + half] = high[8 * half : 8 * half + 8]
    for i in range(12, 16):
        sums[i] = jnp.zeros((8, 128), F32)


def reduce_body(ny, nz, me_y, me_z, pay, out, from_z, from_y, send, receive, meanwhile):
    def along_z(k):
        return (me_y, lax.rem(me_z + k, nz))

    def along_y(k):
        return (lax.rem(me_y + k, ny), me_z)

    def copy(src, dst, sem, to):
        return pltpu.make_async_remote_copy(
            src_ref=src,
            dst_ref=dst,
            send_sem=send.at[sem],
            recv_sem=receive.at[sem],
            device_id=to,
            device_id_type=MESH,
        )

    first = [
        copy(pay.at[lax.rem(me_z + k, nz)], from_z.at[k], k, along_z(k)) for k in range(1, nz)
    ]
    for c in first:
        c.start()
    meanwhile()
    for c in first:
        c.wait()
    total = pay[me_z]
    for k in range(1, nz):
        total = total + from_z[k]
    from_y[me_y] = total
    second = [copy(from_y.at[me_y], from_y.at[me_y], nz + k, along_y(k)) for k in range(1, ny)]
    for c in second:
        c.start()
    for c in second:
        c.wait()
    total = from_y[0]
    for k in range(1, ny):
        total = total + from_y[k]
    out[me_z] = total
    third = [copy(out.at[me_z], out.at[me_z], nz + ny + k, along_z(k)) for k in range(1, nz)]
    for c in third:
        c.start()
    for c in third:
        c.wait()


def finish_body(scale, sums, refined, field, first, bias1, second, bias2, refined_out, field_out):
    refined_out[...] = refined[...]
    field_out[...] = field[...]
    kinds = [jnp.concatenate([sums[2 * i], sums[2 * i + 1]], axis=0) * scale for i in range(6)]
    turned = jnp.concatenate(kinds + [jnp.zeros((32, 128), F32)], axis=0).T
    for x in range(3):
        for y in range(3):
            kind = x if y < 2 else 3 + x
            base = 64 * (y & 1)
            for z in range(3):
                t = (y * 3 + z) * 3 + x
                at = base + 16 * z
                wide = pltpu.roll(kinds[kind], 128 - at, 1) if at else kinds[kind]
                second[t] = wide[:, :16]
                rows = turned[base + 48 + 4 * z : base + 52 + 4 * z]
                rows = jnp.concatenate([rows, rows], axis=0)
                slim = pltpu.roll(rows, 128 - 16 * kind, 1) if kind else rows
                first[t] = slim[:4, :16]
    bias1[...] = turned[60:61, :16]
    bias2[...] = turned[61:62, :16]


def finish(scale, sums, refined, field):
    return pl.pallas_call(
        functools.partial(finish_body, scale),
        out_shape=[
            jax.ShapeDtypeStruct((27, 4, 16), F32),
            jax.ShapeDtypeStruct((1, 16), F32),
            jax.ShapeDtypeStruct((27, 16, 16), F32),
            jax.ShapeDtypeStruct((1, 16), F32),
            jax.ShapeDtypeStruct(refined.shape, refined.dtype),
            jax.ShapeDtypeStruct(field.shape, field.dtype),
        ],
        in_specs=[VMEM] * 3,
        out_specs=[VMEM] * 6,
        name="finish",
    )(sums, refined, field)


GROUPS = 8


def step_body(ny, nz, off, mass, vel, dest, cot, w1, w2, b1, b2, refined, field, sums, *rest):
    (sent, pile, got, part, part16, cext, t1, t2, t2f, t1f, dens, act, ds1, d2, d1, g2, g1, s2, s1) = rest[:19]
    pieces, (pay, from_z, from_y) = rest[19:27], rest[27:30]
    codes, seats, wide, tall, deep = rest[30:35]
    out_all, in_group, out_halo, in_halo, out_sum, in_sum = rest[35:]
    me_y, me_z = lax.axis_index("gy"), lax.axis_index("gz")
    devices = ny * nz
    size = devices // GROUPS
    barrier = pltpu.get_barrier_semaphore()

    def partner(j):
        k = lax.rem(j * 37, devices)
        return (lax.rem(me_y + k // nz, ny), lax.rem(me_z + lax.rem(k, nz), nz))

    def device(a, b):
        return (lax.rem(me_y + a + ny, ny), lax.rem(me_z + b + nz, nz))

    def greet(j, carry):
        pl.semaphore_signal(barrier, inc=1, device_id=partner(j), device_id_type=MESH)
        return carry

    lax.fori_loop(1, devices, greet, 0)

    for y in range(8):
        plane = jnp.swapaxes(cot[:, y].astype(F32), 0, 1).astype(BF)
        tall[y] = plane
        cext[2 + y, 2:10] = plane
    tables_body(w1, w2, t1, t2, t2f, t1f)
    rank_body(2048, dest, codes, seats, devices)
    pack_body(2048, off, mass, vel, codes, seats, sent, pile)

    pl.semaphore_wait(barrier, devices - 1)

    def send(j, carry):
        y, z = partner(j)
        pltpu.make_async_remote_copy(
            src_ref=sent.at[y * nz + z],
            dst_ref=got.at[j],
            send_sem=out_all,
            recv_sem=in_group.at[j // size],
            device_id=(y, z),
            device_id_type=MESH,
        ).start()
        return carry

    lax.fori_loop(1, devices, send, 0)
    got[0] = sent[me_y * nz + me_z]

    def halo(i, src, dst):
        copy = pltpu.make_async_remote_copy(
            src_ref=src,
            dst_ref=dst,
            send_sem=out_halo.at[i],
            recv_sem=in_halo.at[i],
            device_id=device(*AROUND[i % 8]),
            device_id_type=MESH,
        )
        copy.start()
        return copy

    copies = [
        halo(
            8 + i,
            tall.at[pl.ds(*C_FROM[a]), pl.ds(*C_FROM[b])],
            cext.at[pl.ds(C_INTO[a], C_FROM[a][1]), pl.ds(C_INTO[b], C_FROM[b][1])],
        )
        for i, (a, b) in enumerate(AROUND)
    ]

    def landed(first, count, g):
        pltpu.make_async_remote_copy(
            src_ref=sent.at[pl.ds(0, count)],
            dst_ref=got.at[pl.ds(first, count)],
            send_sem=out_all,
            recv_sem=in_group.at[g],
            device_id=device(0, 1),
            device_id_type=MESH,
        ).wait_recv()

    deposit_body(got, part, lambda: landed(1, size - 1, 0), lambda g: landed(g * size, size, g), GROUPS)
    for y in range(9):
        part16[y] = part[y * 40 : (y + 1) * 40].astype(BF)
    copies += [
        halo(i, part16.at[pl.ds(*Y_PART[a]), pl.ds(*Z_PART[b])], pieces[i]) for i, (a, b) in enumerate(AROUND)
    ]
    pltpu.make_async_remote_copy(
        src_ref=sent.at[pl.ds(1, devices - 1)],
        dst_ref=got.at[pl.ds(1, devices - 1)],
        send_sem=out_all,
        recv_sem=in_group.at[0],
        device_id=device(0, 1),
        device_id_type=MESH,
    ).wait_send()
    for c in copies:
        c.wait()

    unet_body(
        ny, nz, me_y, me_z, part, *pieces, cext, t1, t2, t2f, t1f, b1, b2,
        wide, deep, pay, dens, act, ds1, d2, d1, g2, g1, s2, s1,
    )

    def turn():
        for y in range(8):
            refined[:, y] = jnp.swapaxes(wide[y], 0, 1).astype(BF)
            field[:, y] = jnp.swapaxes(deep[y], 0, 1)[:4]

    reduce_body(ny, nz, me_y, me_z, pay, sums, from_z, from_y, out_sum, in_sum, turn)


def whole_step(ny, nz, slots, *args):
    devices = ny * nz
    return pl.pallas_call(
        functools.partial(step_body, ny, nz),
        out_shape=[
            jax.ShapeDtypeStruct((16, 8, 8, 128), BF),
            jax.ShapeDtypeStruct((4, 8, 8, 128), F32),
            jax.ShapeDtypeStruct((nz, 8, 128), F32),
        ],
        in_specs=[VMEM] * 9,
        out_specs=[VMEM] * 3,
        scratch_shapes=[
            pltpu.VMEM((devices, 8, slots), F32),
            pltpu.VMEM((2 * devices, 5 * slots), F32),
            pltpu.VMEM((devices, 8, slots), F32),
            pltpu.VMEM((360, 128), F32),
            pltpu.VMEM((9, 40, 128), BF),
            pltpu.VMEM((12, 12, 16, 128), BF),
            pltpu.VMEM((384, 128), BF),
            pltpu.VMEM((192, 256), BF),
            pltpu.VMEM((192, 256), BF),
            pltpu.VMEM((96, 256), F32),
            pltpu.VMEM((16, 80, 128), BF),
            pltpu.VMEM((14, 16, 16, 128), BF),
            pltpu.VMEM((14, 16, 16, 128), F32),
            pltpu.VMEM((12, 12, 16, 128), BF),
            pltpu.VMEM((10, 10, 16, 128), BF),
            pltpu.VMEM((192, 256), F32),
            pltpu.VMEM((384, 128), F32),
            pltpu.VMEM((16, 128), F32),
            pltpu.VMEM((16, 128), F32),
        ]
        + [pltpu.VMEM((Y_PART[a][1], Z_PART[b][1], 128), BF) for a, b in AROUND]
        + [
            pltpu.VMEM((nz, 8, 128), F32),
            pltpu.VMEM((nz, 8, 128), F32),
            pltpu.VMEM((ny, 8, 128), F32),
            pltpu.VMEM((1, args[0].shape[1]), jnp.int32),
            pltpu.VMEM((1, args[0].shape[1]), jnp.int32),
            pltpu.VMEM((8, 8, 16, 128), F32),
            pltpu.VMEM((8, 8, 16, 128), BF),
            pltpu.VMEM((8, 8, 8, 128), F32),
            pltpu.SemaphoreType.DMA,
            pltpu.SemaphoreType.DMA((GROUPS,)),
            pltpu.SemaphoreType.DMA((16,)),
            pltpu.SemaphoreType.DMA((16,)),
            pltpu.SemaphoreType.DMA((2 * nz + ny,)),
            pltpu.SemaphoreType.DMA((2 * nz + ny,)),
        ],
        compiler_params=pltpu.CompilerParams(collective_id=1, has_side_effects=True, vmem_limit_bytes=LIMIT),
        name="step",
    )(*args)


def local(off, mass, vel, dest, w1, b1, w2, b2, cot):
    ny, nz = lax.axis_size("gy"), lax.axis_size("gz")
    devices = ny * nz
    count = mass.shape[0]
    scale = 1.0 / math.sqrt(8 * 8 * 128 * devices)
    refined, field, sums = whole_step(
        ny,
        nz,
        2 * count // devices,
        off,
        mass.reshape(1, count),
        vel,
        dest.reshape(1, count),
        cot,
        w1.transpose(2, 3, 4, 1, 0).reshape(27, 4, 16),
        w2.transpose(2, 3, 4, 0, 1).reshape(27, 16, 16),
        b1.reshape(1, 16),
        b2.reshape(1, 16),
    )
    first, bias1, second, bias2, refined, field = finish(scale, sums, refined, field)
    return (
        refined,
        field,
        first.reshape(3, 3, 3, 4, 16).transpose(4, 3, 0, 1, 2),
        bias1.reshape(16),
        second.reshape(3, 3, 3, 16, 16).transpose(3, 4, 0, 1, 2),
        bias2.reshape(16),
    )


def solution(mesh):
    placed = (
        P(None, ("gy", "gz")),
        P(("gy", "gz")),
        P(None, ("gy", "gz")),
        P(("gy", "gz"), None),
        P(),
        P(),
        P(),
        P(),
        P(None, "gy", "gz", None),
    )
    return jax.shard_map(
        local,
        mesh=mesh,
        in_specs=placed,
        out_specs=(P(None, "gy", "gz", None), P(None, "gy", "gz", None), P(), P(), P(), P()),
        check_vma=False,
    )
```

```python
import functools
import math

import jax
import jax.numpy as jnp
from jax import lax
from jax.experimental import pallas as pl
from jax.experimental.pallas import tpu as pltpu
from jax.sharding import PartitionSpec as P

F32 = jnp.float32
BF = jnp.bfloat16
MESH = pl.DeviceIdType.MESH
NT = (((1,), (1,)), ((), ()))
TN = (((0,), (0,)), ((), ()))
NN = (((1,), (0,)), ((), ()))
VMEM = pl.BlockSpec(memory_space=pltpu.VMEM)
SMEM = pl.BlockSpec(memory_space=pltpu.SMEM)
LIMIT = 62 * 1024 * 1024


def dot(a, b, dims=NN):
    return lax.dot_general(a, b, dims, preferred_element_type=F32)


def iota(shape, dim):
    return lax.broadcasted_iota(jnp.int32, shape, dim)


def halves(value):
    high = value.astype(BF)
    return high, (value - high.astype(F32)).astype(BF)


def rank_body(chunk, dest, codes, seats, blocks):
    count, width = dest.shape[1], 256
    rows = iota((blocks, chunk), 0)
    before = (iota((width, width), 0) < iota((width, width), 1)).astype(F32).astype(BF)

    def step(k, base):
        here = pl.ds(pl.multiple_of(k * chunk, chunk), chunk)
        to = dest[:, here]
        hot = (rows == to).astype(F32)
        hot16 = hot.astype(BF)
        ranks = []
        for i in range(chunk // width):
            cols = slice(i * width, (i + 1) * width)
            earlier = dot(hot16[:, cols], before) + base
            ranks.append(jnp.sum(hot[:, cols] * earlier, axis=0, keepdims=True))
            base = base + jnp.sum(hot[:, cols], axis=1, keepdims=True)
        rank = jnp.concatenate(ranks, axis=1).astype(jnp.int32)
        codes[:, here] = to + (rank & 1) * blocks
        seats[:, here] = rank >> 1
        return base

    lax.fori_loop(0, count // chunk, step, jnp.zeros((blocks, 1), F32))


def pack_body(chunk, off, mass, vel, codes, seats, out, acc):
    blocks, _, slots = out.shape
    count, half = off.shape[1], slots // 2
    rows = iota((2 * blocks, chunk), 0).astype(F32).astype(BF)
    ranks = iota((half, chunk), 0).astype(F32).astype(BF)
    one, zero = jnp.ones((), BF), jnp.zeros((), BF)
    acc[...] = jnp.zeros_like(acc)

    def step(k, carry):
        here = pl.ds(pl.multiple_of(k * chunk, chunk), chunk)
        hot = jnp.where(rows == codes[:, here].astype(F32).astype(BF), one, zero)
        taken = ranks == seats[:, here].astype(F32).astype(BF)
        spot = off[:, here]
        m = mass[:, here]
        v = vel[:, here]
        planes = (
            halves(spot[2:3] * 128.0)
            + halves(spot[0:1] * 8.0)
            + halves(spot[1:2] * 8.0)
            + (m.astype(BF), (m * v[0:1]).astype(BF), (m * v[1:2]).astype(BF), (m * v[2:3]).astype(BF))
        )
        spread = jnp.concatenate([jnp.where(taken, plane, zero) for plane in planes], axis=0)
        acc[...] += dot(hot, spread, NT)
        return carry

    lax.fori_loop(0, count // chunk, step, 0)
    low_half = iota((blocks, slots), 1) < half

    def plane(i):
        cols = slice(i // 2 * slots, (i // 2 + 1) * slots)
        even, odd = acc[:blocks, cols], acc[blocks:, cols]
        if i % 2:
            return jnp.where(low_half, pltpu.roll(even, half, 1), odd)
        return jnp.where(low_half, even, pltpu.roll(odd, half, 1))

    for i in range(3):
        out[:, i, :] = plane(2 * i) + plane(2 * i + 1)
    out[:, 3, :] = jnp.zeros((blocks, slots), F32)
    for i in range(4):
        out[:, 4 + i, :] = plane(6 + i)


GROUP = 16


def hat(grid, at):
    return jnp.maximum(1.0 - jnp.abs(grid - at), 0.0)


def deposit_body(got, acc, first_ready, ready, groups):
    size = got.shape[0] // groups
    xs = iota((128, 128), 0).astype(F32)
    zs = (iota((40, 128), 0) >> 2).astype(F32)
    ys = iota((16, 128), 0).astype(F32)
    upper = iota((8, 128), 0) >= 4
    acc[...] = jnp.zeros_like(acc)

    def factors(s):
        t = got[s]
        wx = hat(xs, t[0:1]).astype(BF)
        q = jnp.where(upper, t, pltpu.roll(t, 4, 0))
        wzq = hat(zs, t[2:3]) * jnp.concatenate([q] * 5, axis=0)
        wy = hat(ys, t[1:2])
        return wx, jnp.concatenate([wzq * wy[y : y + 1] for y in range(9)], axis=0).astype(BF)

    def add(g):
        for k in range(size // GROUP):
            pairs = [factors(g * size + k * GROUP + i) for i in range(GROUP)]
            right = jnp.concatenate([p[0] for p in pairs], axis=1)
            left = jnp.concatenate([p[1] for p in pairs], axis=1)
            acc[...] += dot(left, right, NT)

    def step(g, carry):
        ready(g)
        add(g)
        return carry

    first_ready()
    add(0)
    lax.fori_loop(1, groups, step, 0)


Y_PART = {1: (4, 5), 0: (0, 9), -1: (0, 4)}
Z_PART = {1: (16, 24), 0: (0, 40), -1: (0, 16)}
AROUND = [(a, b) for a in (1, 0, -1) for b in (1, 0, -1) if (a, b) != (0, 0)]
C_FROM = {1: (6, 2), 0: (0, 8), -1: (0, 2)}
C_INTO = {1: 0, 0: 2, -1: 10}


def tables_body(w1, w2, t1, t2, t2f, t1f):
    lane256, lane128 = iota((16, 256), 1), iota((16, 128), 1)
    rep16 = ((lane256 & 15) == iota((16, 256), 0)).astype(F32).astype(BF)
    rep4 = ((iota((4, 128), 1) & 3) == iota((4, 128), 0)).astype(F32).astype(BF)
    lane8 = iota((8, 256), 1)

    def tap(y, z, x):
        return (y * 3 + z) * 3 + x

    def back(y, z, x):
        return tap(2 - y, 2 - z, 2 - x)

    taps = [(y, z) for y in range(3) for z in range(3)]
    for x in range(3):
        r2 = {(y, z): dot(w2[tap(y, z, x)], rep16) for y, z in taps}
        r2f = {(y, z): dot(w2[back(y, z, x)], rep16, TN) for y, z in taps}
        r1 = {(y, z): dot(w1[tap(y, z, x)], rep4, TN) for y, z in taps}
        r1f = {
            (y, z): jnp.concatenate([dot(w1[back(y, z, x)], rep16), jnp.zeros((4, 256), F32)], axis=0)
            for y, z in taps
        }
        for oy in range(2):
            for oz in range(2):
                a = jnp.zeros((16, 256), F32)
                b = jnp.zeros((16, 256), F32)
                c = jnp.zeros((8, 256), F32)
                for y, z in taps:
                    block = (oy + y) * 4 + oz + z
                    a = jnp.where((lane256 >> 4) == block, r2[y, z], a)
                    b = jnp.where((lane256 >> 4) == block, r2f[y, z], b)
                    c = jnp.where((lane8 >> 4) == block, r1f[y, z], c)
                row = (x * 4 + oy * 2 + oz) * 16
                t2[row : row + 16] = a.astype(BF)
                t2f[row : row + 16] = b.astype(BF)
                t1f[row // 2 : row // 2 + 8] = c
            for oz in range(4):
                a = jnp.zeros((16, 128), F32)
                for y, z in taps:
                    a = jnp.where((lane128 >> 2) == (oy + y) * 8 + oz + z, r1[y, z], a)
                row = (x * 8 + oy * 4 + oz) * 16
                t1[row : row + 16] = a.astype(BF)


def unet_body(
    ny,
    nz,
    gy,
    gz,
    part,
    bl,
    bo,
    br,
    sl,
    sr,
    al,
    ao,
    ar,
    cext,
    t1,
    t2,
    t2f,
    t1f,
    b1,
    b2,
    refined,
    field,
    sums,
    dens,
    act,
    ds1,
    d2,
    d1,
    g2,
    g1,
    s2,
    s1,
):
    lane = iota((128, 128), 1)
    not_first, not_last = lane > 0, lane < 127

    def from_left(v):
        return jnp.where(not_first[: v.shape[0]], pltpu.roll(v, 1, 1), 0.0)

    def from_right(v):
        return jnp.where(not_last[: v.shape[0]], pltpu.roll(v, 127, 1), 0.0)

    def along_x(v, rows, j):
        cols = slice(j * 128, (j + 1) * 128)
        return from_left(v[:rows, cols]) + v[rows : 2 * rows, cols] + from_right(v[2 * rows :, cols])

    zrow = (iota((80, 128), 0) >> 2) - 5 + gz * 8
    z_inside = (zrow >= 0) & (zrow < nz * 8)

    from_side = (gz > 0).astype(F32)
    from_below = (gy > 0).astype(F32)

    def across(left, own, right):
        left, own, right = left.astype(F32), own.astype(F32), right.astype(F32)
        return jnp.concatenate(
            [
                left[0:16],
                own[0:8] + left[16:24] * from_side,
                own[8:32],
                right[0:8] + own[32:40],
                right[8:16],
            ],
            axis=0,
        )

    for y in range(16):
        if y < 4:
            slab = across(bl[y], bo[y], br[y])
        elif y < 12:
            slab = across(sl[y - 4], part[(y - 4) * 40 : (y - 3) * 40], sr[y - 4])
            if y == 4:
                slab = slab + across(bl[4], bo[4], br[4]) * from_below
        else:
            slab = across(al[y - 12], ao[y - 12], ar[y - 12])
            if y == 12:
                slab = slab + across(sl[8], part[320:360], sr[8])
        slab = jnp.concatenate([slab, jnp.zeros((16, 128), F32)], axis=0)
        slab = pltpu.roll(slab, 4, 0)
        at = gy * 8 + (y - 4)
        inside = z_inside & ((at >= 0) & (at < ny * 8))
        dens[y] = jnp.where(inside, slab, 0.0).astype(BF)

    diagonal = iota((16, 16), 0) == iota((16, 16), 1)

    def spread_bias(ref, times):
        column = jnp.sum(jnp.where(diagonal, ref[...], 0.0), axis=1, keepdims=True)
        return jnp.concatenate([jnp.broadcast_to(column, (16, 128))] * times, axis=0)

    bias1, bias2 = spread_bias(b1, 8), spread_bias(b2, 4)

    row1 = iota((128, 128), 0)

    def conv1(by):
        right = jnp.concatenate(
            [
                jnp.concatenate([dens[2 * by + y, 16 * j : 16 * j + 32, :] for y in range(4)], axis=0)
                for j in range(4)
            ],
            axis=1,
        )
        out = dot(t1[...], right)
        yy = gy * 8 + 2 * by - 3 + (row1 >> 6)
        y_in = (yy >= 0) & (yy < ny * 8)
        for j in range(4):
            pre = along_x(out, 128, j) + bias1
            sig = jax.nn.sigmoid(pre)
            zz = gz * 8 + 4 * j - 4 + ((row1 >> 4) & 3)
            inside = y_in & (zz >= 0) & (zz < nz * 8)
            value = jnp.where(inside, pre * sig, 0.0).astype(BF)
            act[pl.ds(2 * by, 2), 4 * j : 4 * j + 4] = value.reshape(2, 4, 16, 128)
            slope = jnp.where(inside, sig * (1.0 + pre * (1.0 - sig)), 0.0)
            ds1[pl.ds(2 * by, 2), 4 * j : 4 * j + 4] = slope.reshape(2, 4, 16, 128)

    for by in range(7):
        conv1(by)

    def block(ref, y0, z0):
        return jnp.concatenate([ref[y0 + y, z0 : z0 + 4].reshape(64, 128) for y in range(4)], axis=0)

    row2 = iota((64, 128), 0)

    def conv2(by):
        right = jnp.concatenate([block(act, 2 * by, 2 * bz + 1) for bz in range(6)], axis=1)
        out = dot(t2[...], right)
        yy = gy * 8 + 2 * by - 2 + (row2 >> 5)
        y_in = (yy >= 0) & (yy < ny * 8)
        for bz in range(6):
            pre = along_x(out, 64, bz) + bias2
            sig = jax.nn.sigmoid(pre)
            zz = gz * 8 + 2 * bz - 2 + ((row2 >> 4) & 1)
            inside = y_in & (zz >= 0) & (zz < nz * 8)
            if 1 <= bz <= 4 and 1 <= by <= 4:
                refined[2 * by - 2 : 2 * by, 2 * bz - 2 : 2 * bz] = (pre * sig).reshape(2, 2, 16, 128)

            cot = cext[pl.ds(2 * by, 2), 2 * bz : 2 * bz + 2].reshape(64, 128).astype(F32)
            delta = jnp.where(inside, cot * (sig * (1.0 + pre * (1.0 - sig))), 0.0)
            d2[pl.ds(2 * by, 2), 2 * bz : 2 * bz + 2] = delta.astype(BF).reshape(2, 2, 16, 128)

    for by in range(6):
        conv2(by)

    def conv3(by):
        right = jnp.concatenate([block(d2, 2 * by, 2 * bz) for bz in range(5)], axis=1)
        out = dot(t2f[...], right)
        for bz in range(5):
            slope = ds1[pl.ds(2 * by + 2, 2), 2 * bz + 3 : 2 * bz + 5].reshape(64, 128)
            delta = along_x(out, 64, bz) * slope
            d1[pl.ds(2 * by, 2), 2 * bz : 2 * bz + 2] = delta.astype(BF).reshape(2, 2, 16, 128)

    for by in range(5):
        conv3(by)

    g2[...] = jnp.zeros_like(g2)
    g1[...] = jnp.zeros_like(g1)
    s2[...] = jnp.zeros_like(s2)
    s1[...] = jnp.zeros_like(s1)
    table4 = t1f[...].astype(BF)

    def last(by):
        right = jnp.concatenate([block(d1, 2 * by, 2 * bz) for bz in range(4)], axis=1)
        out = dot(table4, right)
        for bz in range(4):
            field[pl.ds(2 * by, 2), 2 * bz : 2 * bz + 2] = along_x(out, 32, bz).reshape(2, 2, 8, 128)

        lefts, rights = [], []
        for bz in range(4):
            delta = d2[pl.ds(2 * by + 2, 2), 2 * bz + 2 : 2 * bz + 4].reshape(64, 128).astype(F32)
            s2[...] += delta[0:16] + delta[16:32] + delta[32:48] + delta[48:64]
            lefts.append(
                jnp.concatenate([from_right(delta), delta, from_left(delta)], axis=0).astype(BF)
            )
            rights.append(block(act, 2 * by + 2, 2 * bz + 3))
        g2[...] += dot(jnp.concatenate(lefts, axis=1), jnp.concatenate(rights, axis=1), NT)

        lefts, rights = [], []
        for j in range(2):
            delta = d1[pl.ds(2 * by + 1, 2), 4 * j + 1 : 4 * j + 5].reshape(128, 128).astype(F32)
            total = delta[0:16]
            for i in range(1, 8):
                total = total + delta[16 * i : 16 * i + 16]
            s1[...] += total
            lefts.append(
                jnp.concatenate([from_right(delta), delta, from_left(delta)], axis=0).astype(BF)
            )
            rights.append(
                jnp.concatenate(
                    [dens[2 * by + 3 + y, 16 * j + 16 : 16 * j + 48, :] for y in range(4)], axis=0
                )
            )
        g1[...] += dot(jnp.concatenate(lefts, axis=1), jnp.concatenate(rights, axis=1), NT)

    for by in range(4):
        last(by)

    lane16 = iota((16, 128), 1)
    for x in range(3):
        wide = g2[x * 64 : x * 64 + 16]
        for i in range(1, 4):
            shift = ((i >> 1) * 4 + (i & 1)) * 16
            wide = wide + pltpu.roll(g2[x * 64 + 16 * i : x * 64 + 16 * i + 16], 256 - shift, 1)
        slim = g1[x * 128 : x * 128 + 16]
        for i in range(1, 8):
            shift = (i >> 2) * 32 + (i & 3) * 4
            slim = slim + pltpu.roll(g1[x * 128 + 16 * i : x * 128 + 16 * i + 16], 128 - shift, 1)
        low, high = wide[:, :128], wide[:, 128:]
        free = (lane16 & 63) >= 48
        low = jnp.where(free, jnp.where(lane16 < 64, pltpu.roll(slim, 48, 1), pltpu.roll(slim, 80, 1)), low)
        high = jnp.where(free, pltpu.roll(slim, 112, 1), high)
        if x == 0:
            low = jnp.where(lane16 == 60, jnp.sum(s1[...], axis=1, keepdims=True), low)
            low = jnp.where(lane16 == 61, jnp.sum(s2[...], axis=1, keepdims=True), low)
        for half in range(2):
            sums[2 * x + half] = low[8 * half : 8 * half + 8]
            sums[6 + 2 * x + half] = high[8 * half : 8 * half + 8]
    for i in range(12, 16):
        sums[i] = jnp.zeros((8, 128), F32)


def reduce_body(ny, nz, me_y, me_z, pay, out, from_z, from_y, send, receive, meanwhile):
    def along_z(k):
        return (me_y, lax.rem(me_z + k, nz))

    def along_y(k):
        return (lax.rem(me_y + k, ny), me_z)

    def copy(src, dst, sem, to):
        return pltpu.make_async_remote_copy(
            src_ref=src,
            dst_ref=dst,
            send_sem=send.at[sem],
            recv_sem=receive.at[sem],
            device_id=to,
            device_id_type=MESH,
        )

    first = [
        copy(pay.at[lax.rem(me_z + k, nz)], from_z.at[k], k, along_z(k)) for k in range(1, nz)
    ]
    for c in first:
        c.start()
    meanwhile()
    for c in first:
        c.wait()
    total = pay[me_z]
    for k in range(1, nz):
        total = total + from_z[k]
    from_y[me_y] = total
    second = [copy(from_y.at[me_y], from_y.at[me_y], nz + k, along_y(k)) for k in range(1, ny)]
    for c in second:
        c.start()
    for c in second:
        c.wait()
    total = from_y[0]
    for k in range(1, ny):
        total = total + from_y[k]
    out[me_z] = total
    third = [copy(out.at[me_z], out.at[me_z], nz + ny + k, along_z(k)) for k in range(1, nz)]
    for c in third:
        c.start()
    for c in third:
        c.wait()


def finish_body(scale, sums, refined, field, first, bias1, second, bias2, refined_out, field_out):
    refined_out[...] = refined[...]
    field_out[...] = field[...]
    kinds = [jnp.concatenate([sums[2 * i], sums[2 * i + 1]], axis=0) * scale for i in range(6)]
    turned = jnp.concatenate(kinds + [jnp.zeros((32, 128), F32)], axis=0).T
    for x in range(3):
        for y in range(3):
            kind = x if y < 2 else 3 + x
            base = 64 * (y & 1)
            for z in range(3):
                t = (y * 3 + z) * 3 + x
                at = base + 16 * z
                wide = pltpu.roll(kinds[kind], 128 - at, 1) if at else kinds[kind]
                second[t] = wide[:, :16]
                rows = turned[base + 48 + 4 * z : base + 52 + 4 * z]
                rows = jnp.concatenate([rows, rows], axis=0)
                slim = pltpu.roll(rows, 128 - 16 * kind, 1) if kind else rows
                first[t] = slim[:4, :16]
    bias1[...] = turned[60:61, :16]
    bias2[...] = turned[61:62, :16]


def finish(scale, sums, refined, field):
    return pl.pallas_call(
        functools.partial(finish_body, scale),
        out_shape=[
            jax.ShapeDtypeStruct((27, 4, 16), F32),
            jax.ShapeDtypeStruct((1, 16), F32),
            jax.ShapeDtypeStruct((27, 16, 16), F32),
            jax.ShapeDtypeStruct((1, 16), F32),
            jax.ShapeDtypeStruct(refined.shape, refined.dtype),
            jax.ShapeDtypeStruct(field.shape, field.dtype),
        ],
        in_specs=[VMEM] * 3,
        out_specs=[VMEM] * 6,
        name="finish",
    )(sums, refined, field)


GROUPS = 8


def step_body(ny, nz, off, mass, vel, dest, cot, w1, w2, b1, b2, refined, field, sums, *rest):
    (sent, pile, got, part, part16, cext, t1, t2, t2f, t1f, dens, act, ds1, d2, d1, g2, g1, s2, s1) = rest[:19]
    pieces, (pay, from_z, from_y) = rest[19:27], rest[27:30]
    codes, seats, wide, tall, deep = rest[30:35]
    out_all, in_group, out_halo, in_halo, out_sum, in_sum, rows_in = rest[35:]
    me_y, me_z = lax.axis_index("gy"), lax.axis_index("gz")
    devices = ny * nz
    size = devices // GROUPS
    barrier = pltpu.get_barrier_semaphore()

    def partner(j):
        k = lax.rem(j * 37, devices)
        return (lax.rem(me_y + k // nz, ny), lax.rem(me_z + lax.rem(k, nz), nz))

    def device(a, b):
        return (lax.rem(me_y + a + ny, ny), lax.rem(me_z + b + nz, nz))

    row = [(me_y, lax.rem(me_z + k, nz)) for k in range(1, nz)]
    column = [(lax.rem(me_y + k, ny), me_z) for k in range(1, ny)]
    for to in row + column:
        pl.semaphore_signal(barrier, inc=1, device_id=to, device_id_type=MESH)

    for y in range(8):
        plane = jnp.swapaxes(cot[:, y].astype(F32), 0, 1).astype(BF)
        tall[y] = plane
        cext[2 + y, 2:10] = plane
    tables_body(w1, w2, t1, t2, t2f, t1f)
    pl.semaphore_wait(barrier, nz + ny - 2)
    for to in column:
        pl.semaphore_signal(rows_in, inc=1, device_id=to, device_id_type=MESH)
    rank_body(2048, dest, codes, seats, devices)
    pack_body(2048, off, mass, vel, codes, seats, sent, pile)

    pl.semaphore_wait(rows_in, ny - 1)

    def send(j, carry):
        y, z = partner(j)
        pltpu.make_async_remote_copy(
            src_ref=sent.at[y * nz + z],
            dst_ref=got.at[j],
            send_sem=out_all,
            recv_sem=in_group.at[j // size],
            device_id=(y, z),
            device_id_type=MESH,
        ).start()
        return carry

    lax.fori_loop(1, devices, send, 0)
    got[0] = sent[me_y * nz + me_z]

    def halo(i, src, dst):
        copy = pltpu.make_async_remote_copy(
            src_ref=src,
            dst_ref=dst,
            send_sem=out_halo.at[i],
            recv_sem=in_halo.at[i],
            device_id=device(*AROUND[i % 8]),
            device_id_type=MESH,
        )
        copy.start()
        return copy

    copies = [
        halo(
            8 + i,
            tall.at[pl.ds(*C_FROM[a]), pl.ds(*C_FROM[b])],
            cext.at[pl.ds(C_INTO[a], C_FROM[a][1]), pl.ds(C_INTO[b], C_FROM[b][1])],
        )
        for i, (a, b) in enumerate(AROUND)
    ]

    def landed(first, count, g):
        pltpu.make_async_remote_copy(
            src_ref=sent.at[pl.ds(0, count)],
            dst_ref=got.at[pl.ds(first, count)],
            send_sem=out_all,
            recv_sem=in_group.at[g],
            device_id=device(0, 1),
            device_id_type=MESH,
        ).wait_recv()

    deposit_body(got, part, lambda: landed(1, size - 1, 0), lambda g: landed(g * size, size, g), GROUPS)
    for y in range(9):
        part16[y] = part[y * 40 : (y + 1) * 40].astype(BF)
    copies += [
        halo(i, part16.at[pl.ds(*Y_PART[a]), pl.ds(*Z_PART[b])], pieces[i]) for i, (a, b) in enumerate(AROUND)
    ]
    pltpu.make_async_remote_copy(
        src_ref=sent.at[pl.ds(1, devices - 1)],
        dst_ref=got.at[pl.ds(1, devices - 1)],
        send_sem=out_all,
        recv_sem=in_group.at[0],
        device_id=device(0, 1),
        device_id_type=MESH,
    ).wait_send()
    for c in copies:
        c.wait()

    unet_body(
        ny, nz, me_y, me_z, part, *pieces, cext, t1, t2, t2f, t1f, b1, b2,
        wide, deep, pay, dens, act, ds1, d2, d1, g2, g1, s2, s1,
    )

    def turn():
        for y in range(8):
            refined[:, y] = jnp.swapaxes(wide[y], 0, 1).astype(BF)
            field[:, y] = jnp.swapaxes(deep[y], 0, 1)[:4]

    reduce_body(ny, nz, me_y, me_z, pay, sums, from_z, from_y, out_sum, in_sum, turn)


def whole_step(ny, nz, slots, *args):
    devices = ny * nz
    return pl.pallas_call(
        functools.partial(step_body, ny, nz),
        out_shape=[
            jax.ShapeDtypeStruct((16, 8, 8, 128), BF),
            jax.ShapeDtypeStruct((4, 8, 8, 128), F32),
            jax.ShapeDtypeStruct((nz, 8, 128), F32),
        ],
        in_specs=[VMEM] * 9,
        out_specs=[VMEM] * 3,
        scratch_shapes=[
            pltpu.VMEM((devices, 8, slots), F32),
            pltpu.VMEM((2 * devices, 5 * slots), F32),
            pltpu.VMEM((devices, 8, slots), F32),
            pltpu.VMEM((360, 128), F32),
            pltpu.VMEM((9, 40, 128), BF),
            pltpu.VMEM((12, 12, 16, 128), BF),
            pltpu.VMEM((384, 128), BF),
            pltpu.VMEM((192, 256), BF),
            pltpu.VMEM((192, 256), BF),
            pltpu.VMEM((96, 256), F32),
            pltpu.VMEM((16, 80, 128), BF),
            pltpu.VMEM((14, 16, 16, 128), BF),
            pltpu.VMEM((14, 16, 16, 128), F32),
            pltpu.VMEM((12, 12, 16, 128), BF),
            pltpu.VMEM((10, 10, 16, 128), BF),
            pltpu.VMEM((192, 256), F32),
            pltpu.VMEM((384, 128), F32),
            pltpu.VMEM((16, 128), F32),
            pltpu.VMEM((16, 128), F32),
        ]
        + [pltpu.VMEM((Y_PART[a][1], Z_PART[b][1], 128), BF) for a, b in AROUND]
        + [
            pltpu.VMEM((nz, 8, 128), F32),
            pltpu.VMEM((nz, 8, 128), F32),
            pltpu.VMEM((ny, 8, 128), F32),
            pltpu.VMEM((1, args[0].shape[1]), jnp.int32),
            pltpu.VMEM((1, args[0].shape[1]), jnp.int32),
            pltpu.VMEM((8, 8, 16, 128), F32),
            pltpu.VMEM((8, 8, 16, 128), BF),
            pltpu.VMEM((8, 8, 8, 128), F32),
            pltpu.SemaphoreType.DMA,
            pltpu.SemaphoreType.DMA((GROUPS,)),
            pltpu.SemaphoreType.DMA((16,)),
            pltpu.SemaphoreType.DMA((16,)),
            pltpu.SemaphoreType.DMA((2 * nz + ny,)),
            pltpu.SemaphoreType.DMA((2 * nz + ny,)),
            pltpu.SemaphoreType.REGULAR,
        ],
        compiler_params=pltpu.CompilerParams(collective_id=1, has_side_effects=True, vmem_limit_bytes=LIMIT),
        name="step",
    )(*args)


def local(off, mass, vel, dest, w1, b1, w2, b2, cot):
    ny, nz = lax.axis_size("gy"), lax.axis_size("gz")
    devices = ny * nz
    count = mass.shape[0]
    scale = 1.0 / math.sqrt(8 * 8 * 128 * devices)
    refined, field, sums = whole_step(
        ny,
        nz,
        2 * count // devices,
        off,
        mass.reshape(1, count),
        vel,
        dest.reshape(1, count),
        cot,
        w1.transpose(2, 3, 4, 1, 0).reshape(27, 4, 16),
        w2.transpose(2, 3, 4, 0, 1).reshape(27, 16, 16),
        b1.reshape(1, 16),
        b2.reshape(1, 16),
    )
    first, bias1, second, bias2, refined, field = finish(scale, sums, refined, field)
    return (
        refined,
        field,
        first.reshape(3, 3, 3, 4, 16).transpose(4, 3, 0, 1, 2),
        bias1.reshape(16),
        second.reshape(3, 3, 3, 16, 16).transpose(3, 4, 0, 1, 2),
        bias2.reshape(16),
    )


def solution(mesh):
    placed = (
        P(None, ("gy", "gz")),
        P(("gy", "gz")),
        P(None, ("gy", "gz")),
        P(("gy", "gz"), None),
        P(),
        P(),
        P(),
        P(),
        P(None, "gy", "gz", None),
    )
    return jax.shard_map(
        local,
        mesh=mesh,
        in_specs=placed,
        out_specs=(P(None, "gy", "gz", None), P(None, "gy", "gz", None), P(), P(), P(), P()),
        check_vma=False,
    )
```

```python
import functools
import math

import jax
import jax.numpy as jnp
from jax import lax
from jax.experimental import pallas as pl
from jax.experimental.pallas import tpu as pltpu
from jax.sharding import PartitionSpec as P

F32 = jnp.float32
BF = jnp.bfloat16
MESH = pl.DeviceIdType.MESH
NT = (((1,), (1,)), ((), ()))
TN = (((0,), (0,)), ((), ()))
NN = (((1,), (0,)), ((), ()))
VMEM = pl.BlockSpec(memory_space=pltpu.VMEM)
SMEM = pl.BlockSpec(memory_space=pltpu.SMEM)
LIMIT = 62 * 1024 * 1024


def dot(a, b, dims=NN):
    return lax.dot_general(a, b, dims, preferred_element_type=F32)


def iota(shape, dim):
    return lax.broadcasted_iota(jnp.int32, shape, dim)


def halves(value):
    high = value.astype(BF)
    return high, (value - high.astype(F32)).astype(BF)


def rank_body(chunk, dest, codes, seats, blocks):
    count, width = dest.shape[1], 256
    rows = iota((blocks, chunk), 0)
    before = (iota((width, width), 0) < iota((width, width), 1)).astype(F32).astype(BF)

    def step(k, base):
        here = pl.ds(pl.multiple_of(k * chunk, chunk), chunk)
        to = dest[:, here]
        hot = (rows == to).astype(F32)
        hot16 = hot.astype(BF)
        ranks = []
        for i in range(chunk // width):
            cols = slice(i * width, (i + 1) * width)
            earlier = dot(hot16[:, cols], before) + base
            ranks.append(jnp.sum(hot[:, cols] * earlier, axis=0, keepdims=True))
            base = base + jnp.sum(hot[:, cols], axis=1, keepdims=True)
        rank = jnp.concatenate(ranks, axis=1).astype(jnp.int32)
        codes[:, here] = to + (rank & 1) * blocks
        seats[:, here] = rank >> 1
        return base

    lax.fori_loop(0, count // chunk, step, jnp.zeros((blocks, 1), F32))


def pack_body(chunk, off, mass, vel, codes, seats, out, acc):
    blocks, _, slots = out.shape
    count, half = off.shape[1], slots // 2
    rows = iota((2 * blocks, chunk), 0).astype(F32).astype(BF)
    ranks = iota((half, chunk), 0).astype(F32).astype(BF)
    one, zero = jnp.ones((), BF), jnp.zeros((), BF)
    acc[...] = jnp.zeros_like(acc)

    def step(k, carry):
        here = pl.ds(pl.multiple_of(k * chunk, chunk), chunk)
        hot = jnp.where(rows == codes[:, here].astype(F32).astype(BF), one, zero)
        taken = ranks == seats[:, here].astype(F32).astype(BF)
        spot = off[:, here]
        m = mass[:, here]
        v = vel[:, here]
        planes = (
            halves(spot[2:3] * 128.0)
            + halves(spot[0:1] * 8.0)
            + halves(spot[1:2] * 8.0)
            + (m.astype(BF), (m * v[0:1]).astype(BF), (m * v[1:2]).astype(BF), (m * v[2:3]).astype(BF))
        )
        spread = jnp.concatenate([jnp.where(taken, plane, zero) for plane in planes], axis=0)
        acc[...] += dot(hot, spread, NT)
        return carry

    lax.fori_loop(0, count // chunk, step, 0)
    low_half = iota((blocks, slots), 1) < half

    def plane(i):
        cols = slice(i // 2 * slots, (i // 2 + 1) * slots)
        even, odd = acc[:blocks, cols], acc[blocks:, cols]
        if i % 2:
            return jnp.where(low_half, pltpu.roll(even, half, 1), odd)
        return jnp.where(low_half, even, pltpu.roll(odd, half, 1))

    for i in range(3):
        out[:, i, :] = plane(2 * i) + plane(2 * i + 1)
    out[:, 3, :] = jnp.zeros((blocks, slots), F32)
    for i in range(4):
        out[:, 4 + i, :] = plane(6 + i)


GROUP = 16


def hat(grid, at):
    return jnp.maximum(1.0 - jnp.abs(grid - at), 0.0)


def deposit_body(got, acc, first_ready, ready, groups):
    size = got.shape[0] // groups
    xs = iota((128, 128), 0).astype(F32)
    zs = (iota((40, 128), 0) >> 2).astype(F32)
    ys = iota((16, 128), 0).astype(F32)
    upper = iota((8, 128), 0) >= 4
    acc[...] = jnp.zeros_like(acc)

    def factors(s):
        t = got[s]
        wx = hat(xs, t[0:1]).astype(BF)
        q = jnp.where(upper, t, pltpu.roll(t, 4, 0))
        wzq = hat(zs, t[2:3]) * jnp.concatenate([q] * 5, axis=0)
        wy = hat(ys, t[1:2])
        return wx, jnp.concatenate([wzq * wy[y : y + 1] for y in range(9)], axis=0).astype(BF)

    def add(g):
        for k in range(size // GROUP):
            pairs = [factors(g * size + k * GROUP + i) for i in range(GROUP)]
            right = jnp.concatenate([p[0] for p in pairs], axis=1)
            left = jnp.concatenate([p[1] for p in pairs], axis=1)
            acc[...] += dot(left, right, NT)

    def step(g, carry):
        ready(g)
        add(g)
        return carry

    first_ready()
    add(0)
    lax.fori_loop(1, groups, step, 0)


Y_PART = {1: (4, 5), 0: (0, 9), -1: (0, 4)}
Z_PART = {1: (16, 24), 0: (0, 40), -1: (0, 16)}
AROUND = [(a, b) for a in (1, 0, -1) for b in (1, 0, -1) if (a, b) != (0, 0)]
C_FROM = {1: (6, 2), 0: (0, 8), -1: (0, 2)}
C_INTO = {1: 0, 0: 2, -1: 10}


def tables_body(w1, w2, t1, t2, t2f, t1f):
    lane256, lane128 = iota((16, 256), 1), iota((16, 128), 1)
    rep16 = ((lane256 & 15) == iota((16, 256), 0)).astype(F32).astype(BF)
    rep4 = ((iota((4, 128), 1) & 3) == iota((4, 128), 0)).astype(F32).astype(BF)
    lane8 = iota((8, 256), 1)

    def tap(y, z, x):
        return (y * 3 + z) * 3 + x

    def back(y, z, x):
        return tap(2 - y, 2 - z, 2 - x)

    taps = [(y, z) for y in range(3) for z in range(3)]
    for x in range(3):
        r2 = {(y, z): dot(w2[tap(y, z, x)], rep16) for y, z in taps}
        r2f = {(y, z): dot(w2[back(y, z, x)], rep16, TN) for y, z in taps}
        r1 = {(y, z): dot(w1[tap(y, z, x)], rep4, TN) for y, z in taps}
        r1f = {
            (y, z): jnp.concatenate([dot(w1[back(y, z, x)], rep16), jnp.zeros((4, 256), F32)], axis=0)
            for y, z in taps
        }
        for oy in range(2):
            for oz in range(2):
                a = jnp.zeros((16, 256), F32)
                b = jnp.zeros((16, 256), F32)
                c = jnp.zeros((8, 256), F32)
                for y, z in taps:
                    block = (oy + y) * 4 + oz + z
                    a = jnp.where((lane256 >> 4) == block, r2[y, z], a)
                    b = jnp.where((lane256 >> 4) == block, r2f[y, z], b)
                    c = jnp.where((lane8 >> 4) == block, r1f[y, z], c)
                row = (x * 4 + oy * 2 + oz) * 16
                t2[row : row + 16] = a.astype(BF)
                t2f[row : row + 16] = b.astype(BF)
                t1f[row // 2 : row // 2 + 8] = c
            for oz in range(4):
                a = jnp.zeros((16, 128), F32)
                for y, z in taps:
                    a = jnp.where((lane128 >> 2) == (oy + y) * 8 + oz + z, r1[y, z], a)
                row = (x * 8 + oy * 4 + oz) * 16
                t1[row : row + 16] = a.astype(BF)


def unet_body(
    ny,
    nz,
    gy,
    gz,
    part,
    bl,
    bo,
    br,
    sl,
    sr,
    al,
    ao,
    ar,
    cext,
    t1,
    t2,
    t2f,
    t1f,
    b1,
    b2,
    refined,
    field,
    sums,
    dens,
    act,
    ds1,
    d2,
    d1,
    g2,
    g1,
    s2,
    s1,
):
    lane = iota((128, 128), 1)
    not_first, not_last = lane > 0, lane < 127

    def from_left(v):
        return jnp.where(not_first[: v.shape[0]], pltpu.roll(v, 1, 1), 0.0)

    def from_right(v):
        return jnp.where(not_last[: v.shape[0]], pltpu.roll(v, 127, 1), 0.0)

    def along_x(v, rows, j):
        cols = slice(j * 128, (j + 1) * 128)
        return from_left(v[:rows, cols]) + v[rows : 2 * rows, cols] + from_right(v[2 * rows :, cols])

    zrow = (iota((80, 128), 0) >> 2) - 5 + gz * 8
    z_inside = (zrow >= 0) & (zrow < nz * 8)

    from_side = (gz > 0).astype(F32)
    from_below = (gy > 0).astype(F32)

    def across(left, own, right):
        left, own, right = left.astype(F32), own.astype(F32), right.astype(F32)
        return jnp.concatenate(
            [
                left[0:16],
                own[0:8] + left[16:24] * from_side,
                own[8:32],
                right[0:8] + own[32:40],
                right[8:16],
            ],
            axis=0,
        )

    for y in range(16):
        if y < 4:
            slab = across(bl[y], bo[y], br[y])
        elif y < 12:
            slab = across(sl[y - 4], part[(y - 4) * 40 : (y - 3) * 40], sr[y - 4])
            if y == 4:
                slab = slab + across(bl[4], bo[4], br[4]) * from_below
        else:
            slab = across(al[y - 12], ao[y - 12], ar[y - 12])
            if y == 12:
                slab = slab + across(sl[8], part[320:360], sr[8])
        slab = jnp.concatenate([slab, jnp.zeros((16, 128), F32)], axis=0)
        slab = pltpu.roll(slab, 4, 0)
        at = gy * 8 + (y - 4)
        inside = z_inside & ((at >= 0) & (at < ny * 8))
        dens[y] = jnp.where(inside, slab, 0.0).astype(BF)

    diagonal = iota((16, 16), 0) == iota((16, 16), 1)

    def spread_bias(ref, times):
        column = jnp.sum(jnp.where(diagonal, ref[...], 0.0), axis=1, keepdims=True)
        return jnp.concatenate([jnp.broadcast_to(column, (16, 128))] * times, axis=0)

    bias1, bias2 = spread_bias(b1, 8), spread_bias(b2, 4)

    row1 = iota((128, 128), 0)

    def conv1(by):
        right = jnp.concatenate(
            [
                jnp.concatenate([dens[2 * by + y, 16 * j : 16 * j + 32, :] for y in range(4)], axis=0)
                for j in range(4)
            ],
            axis=1,
        )
        out = dot(t1[...], right)
        yy = gy * 8 + 2 * by - 3 + (row1 >> 6)
        y_in = (yy >= 0) & (yy < ny * 8)
        for j in range(4):
            pre = along_x(out, 128, j) + bias1
            sig = jax.nn.sigmoid(pre)
            zz = gz * 8 + 4 * j - 4 + ((row1 >> 4) & 3)
            inside = y_in & (zz >= 0) & (zz < nz * 8)
            value = jnp.where(inside, pre * sig, 0.0).astype(BF)
            act[pl.ds(2 * by, 2), 4 * j : 4 * j + 4] = value.reshape(2, 4, 16, 128)
            slope = jnp.where(inside, sig * (1.0 + pre * (1.0 - sig)), 0.0)
            ds1[pl.ds(2 * by, 2), 4 * j : 4 * j + 4] = slope.reshape(2, 4, 16, 128)

    for by in range(7):
        conv1(by)

    def block(ref, y0, z0):
        return jnp.concatenate([ref[y0 + y, z0 : z0 + 4].reshape(64, 128) for y in range(4)], axis=0)

    row2 = iota((64, 128), 0)

    def conv2(by):
        right = jnp.concatenate([block(act, 2 * by, 2 * bz + 1) for bz in range(6)], axis=1)
        out = dot(t2[...], right)
        yy = gy * 8 + 2 * by - 2 + (row2 >> 5)
        y_in = (yy >= 0) & (yy < ny * 8)
        for bz in range(6):
            pre = along_x(out, 64, bz) + bias2
            sig = jax.nn.sigmoid(pre)
            zz = gz * 8 + 2 * bz - 2 + ((row2 >> 4) & 1)
            inside = y_in & (zz >= 0) & (zz < nz * 8)
            if 1 <= bz <= 4 and 1 <= by <= 4:
                refined[2 * by - 2 : 2 * by, 2 * bz - 2 : 2 * bz] = (pre * sig).reshape(2, 2, 16, 128)

            cot = cext[pl.ds(2 * by, 2), 2 * bz : 2 * bz + 2].reshape(64, 128).astype(F32)
            delta = jnp.where(inside, cot * (sig * (1.0 + pre * (1.0 - sig))), 0.0)
            d2[pl.ds(2 * by, 2), 2 * bz : 2 * bz + 2] = delta.astype(BF).reshape(2, 2, 16, 128)

    for by in range(6):
        conv2(by)

    def conv3(by):
        right = jnp.concatenate([block(d2, 2 * by, 2 * bz) for bz in range(5)], axis=1)
        out = dot(t2f[...], right)
        for bz in range(5):
            slope = ds1[pl.ds(2 * by + 2, 2), 2 * bz + 3 : 2 * bz + 5].reshape(64, 128)
            delta = along_x(out, 64, bz) * slope
            d1[pl.ds(2 * by, 2), 2 * bz : 2 * bz + 2] = delta.astype(BF).reshape(2, 2, 16, 128)

    for by in range(5):
        conv3(by)

    g2[...] = jnp.zeros_like(g2)
    g1[...] = jnp.zeros_like(g1)
    s2[...] = jnp.zeros_like(s2)
    s1[...] = jnp.zeros_like(s1)
    table4 = t1f[...].astype(BF)

    def last(by):
        right = jnp.concatenate([block(d1, 2 * by, 2 * bz) for bz in range(4)], axis=1)
        out = dot(table4, right)
        for bz in range(4):
            field[pl.ds(2 * by, 2), 2 * bz : 2 * bz + 2] = along_x(out, 32, bz).reshape(2, 2, 8, 128)

        lefts, rights = [], []
        for bz in range(4):
            delta = d2[pl.ds(2 * by + 2, 2), 2 * bz + 2 : 2 * bz + 4].reshape(64, 128).astype(F32)
            s2[...] += delta[0:16] + delta[16:32] + delta[32:48] + delta[48:64]
            lefts.append(
                jnp.concatenate([from_right(delta), delta, from_left(delta)], axis=0).astype(BF)
            )
            rights.append(block(act, 2 * by + 2, 2 * bz + 3))
        g2[...] += dot(jnp.concatenate(lefts, axis=1), jnp.concatenate(rights, axis=1), NT)

        lefts, rights = [], []
        for j in range(2):
            delta = d1[pl.ds(2 * by + 1, 2), 4 * j + 1 : 4 * j + 5].reshape(128, 128).astype(F32)
            total = delta[0:16]
            for i in range(1, 8):
                total = total + delta[16 * i : 16 * i + 16]
            s1[...] += total
            lefts.append(
                jnp.concatenate([from_right(delta), delta, from_left(delta)], axis=0).astype(BF)
            )
            rights.append(
                jnp.concatenate(
                    [dens[2 * by + 3 + y, 16 * j + 16 : 16 * j + 48, :] for y in range(4)], axis=0
                )
            )
        g1[...] += dot(jnp.concatenate(lefts, axis=1), jnp.concatenate(rights, axis=1), NT)

    for by in range(4):
        last(by)

    lane16 = iota((16, 128), 1)
    for x in range(3):
        wide = g2[x * 64 : x * 64 + 16]
        for i in range(1, 4):
            shift = ((i >> 1) * 4 + (i & 1)) * 16
            wide = wide + pltpu.roll(g2[x * 64 + 16 * i : x * 64 + 16 * i + 16], 256 - shift, 1)
        slim = g1[x * 128 : x * 128 + 16]
        for i in range(1, 8):
            shift = (i >> 2) * 32 + (i & 3) * 4
            slim = slim + pltpu.roll(g1[x * 128 + 16 * i : x * 128 + 16 * i + 16], 128 - shift, 1)
        low, high = wide[:, :128], wide[:, 128:]
        free = (lane16 & 63) >= 48
        low = jnp.where(free, jnp.where(lane16 < 64, pltpu.roll(slim, 48, 1), pltpu.roll(slim, 80, 1)), low)
        high = jnp.where(free, pltpu.roll(slim, 112, 1), high)
        if x == 0:
            low = jnp.where(lane16 == 60, jnp.sum(s1[...], axis=1, keepdims=True), low)
            low = jnp.where(lane16 == 61, jnp.sum(s2[...], axis=1, keepdims=True), low)
        sums[x] = low
        sums[3 + x] = high
    sums[6] = jnp.zeros((16, 128), F32)
    sums[7] = jnp.zeros((16, 128), F32)


FAR_ROW = sorted(range(1, 16), key=lambda k: -min(k // 4, 4 - k // 4) - min(k % 4, 4 - k % 4))


def reduce_body(ny, nz, me_y, me_z, pay, out, from_z, from_y, send, receive, meanwhile):
    def along_z(k):
        return (me_y, lax.rem(me_z + k, nz))

    def along_y(k):
        return (lax.rem(me_y + k, ny), me_z)

    def copy(src, dst, sem, to):
        return pltpu.make_async_remote_copy(
            src_ref=src,
            dst_ref=dst,
            send_sem=send.at[sem],
            recv_sem=receive.at[sem],
            device_id=to,
            device_id_type=MESH,
        )

    first = [copy(pay.at[lax.rem(me_y + k, ny)], from_y.at[k], k, along_y(k)) for k in range(1, ny)]
    for c in first:
        c.start()
    meanwhile()
    for c in first:
        c.wait()
    total = pay[me_y]
    for k in range(1, ny):
        total = total + from_y[k]
    from_z[me_z] = total
    second = [copy(from_z.at[me_z], from_z.at[me_z], ny + k, along_z(k)) for k in FAR_ROW]
    for c in second:
        c.start()
    for c in second:
        c.wait()
    total = from_z[0]
    for k in range(1, nz):
        total = total + from_z[k]
    out[me_y] = total
    third = [copy(out.at[me_y], out.at[me_y], nz + ny + k, along_y(k)) for k in range(1, ny)]
    for c in third:
        c.start()
    for c in third:
        c.wait()


def finish_body(scale, sums, refined, field, first, bias1, second, bias2, refined_out, field_out):
    refined_out[...] = refined[...]
    field_out[...] = field[...]
    kinds = [sums[i] * scale for i in range(6)]
    turned = jnp.concatenate(kinds + [jnp.zeros((32, 128), F32)], axis=0).T
    for x in range(3):
        for y in range(3):
            kind = x if y < 2 else 3 + x
            base = 64 * (y & 1)
            for z in range(3):
                t = (y * 3 + z) * 3 + x
                at = base + 16 * z
                wide = pltpu.roll(kinds[kind], 128 - at, 1) if at else kinds[kind]
                second[t] = wide[:, :16]
                rows = turned[base + 48 + 4 * z : base + 52 + 4 * z]
                rows = jnp.concatenate([rows, rows], axis=0)
                slim = pltpu.roll(rows, 128 - 16 * kind, 1) if kind else rows
                first[t] = slim[:4, :16]
    bias1[...] = turned[60:61, :16]
    bias2[...] = turned[61:62, :16]


def finish(scale, sums, refined, field):
    return pl.pallas_call(
        functools.partial(finish_body, scale),
        out_shape=[
            jax.ShapeDtypeStruct((27, 4, 16), F32),
            jax.ShapeDtypeStruct((1, 16), F32),
            jax.ShapeDtypeStruct((27, 16, 16), F32),
            jax.ShapeDtypeStruct((1, 16), F32),
            jax.ShapeDtypeStruct(refined.shape, refined.dtype),
            jax.ShapeDtypeStruct(field.shape, field.dtype),
        ],
        in_specs=[VMEM] * 3,
        out_specs=[VMEM] * 6,
        name="finish",
    )(sums, refined, field)


GROUPS = 8


def step_body(ny, nz, off, mass, vel, dest, cot, w1, w2, b1, b2, refined, field, sums, *rest):
    (sent, pile, got, part, part16, cext, t1, t2, t2f, t1f, dens, act, ds1, d2, d1, g2, g1, s2, s1) = rest[:19]
    pieces, (pay, from_z, from_y) = rest[19:27], rest[27:30]
    codes, seats, wide, tall, deep = rest[30:35]
    out_all, in_group, out_halo, in_halo, out_sum, in_sum, rows_in = rest[35:]
    me_y, me_z = lax.axis_index("gy"), lax.axis_index("gz")
    devices = ny * nz
    size = devices // GROUPS
    barrier = pltpu.get_barrier_semaphore()

    def partner(j):
        k = lax.rem(j * 37, devices)
        return (lax.rem(me_y + k // nz, ny), lax.rem(me_z + lax.rem(k, nz), nz))

    def device(a, b):
        return (lax.rem(me_y + a + ny, ny), lax.rem(me_z + b + nz, nz))

    row = [(me_y, lax.rem(me_z + k, nz)) for k in range(1, nz)]
    column = [(lax.rem(me_y + k, ny), me_z) for k in range(1, ny)]
    for to in row + column:
        pl.semaphore_signal(barrier, inc=1, device_id=to, device_id_type=MESH)

    rank_body(2048, dest, codes, seats, devices)
    pl.semaphore_wait(barrier, nz + ny - 2)
    for to in column:
        pl.semaphore_signal(rows_in, inc=1, device_id=to, device_id_type=MESH)
    pack_body(2048, off, mass, vel, codes, seats, sent, pile)

    pl.semaphore_wait(rows_in, ny - 1)

    def send(j, carry):
        y, z = partner(j)
        pltpu.make_async_remote_copy(
            src_ref=sent.at[y * nz + z],
            dst_ref=got.at[j],
            send_sem=out_all,
            recv_sem=in_group.at[j // size],
            device_id=(y, z),
            device_id_type=MESH,
        ).start()
        return carry

    lax.fori_loop(1, devices, send, 0)
    got[0] = sent[me_y * nz + me_z]

    for y in range(8):
        plane = jnp.swapaxes(cot[:, y].astype(F32), 0, 1).astype(BF)
        tall[y] = plane
        cext[2 + y, 2:10] = plane

    def halo(i, src, dst):
        copy = pltpu.make_async_remote_copy(
            src_ref=src,
            dst_ref=dst,
            send_sem=out_halo.at[i],
            recv_sem=in_halo.at[i],
            device_id=device(*AROUND[i % 8]),
            device_id_type=MESH,
        )
        copy.start()
        return copy

    copies = [
        halo(
            8 + i,
            tall.at[pl.ds(*C_FROM[a]), pl.ds(*C_FROM[b])],
            cext.at[pl.ds(C_INTO[a], C_FROM[a][1]), pl.ds(C_INTO[b], C_FROM[b][1])],
        )
        for i, (a, b) in enumerate(AROUND)
    ]

    tables_body(w1, w2, t1, t2, t2f, t1f)

    def landed(first, count, g):
        pltpu.make_async_remote_copy(
            src_ref=sent.at[pl.ds(0, count)],
            dst_ref=got.at[pl.ds(first, count)],
            send_sem=out_all,
            recv_sem=in_group.at[g],
            device_id=device(0, 1),
            device_id_type=MESH,
        ).wait_recv()

    deposit_body(got, part, lambda: landed(1, size - 1, 0), lambda g: landed(g * size, size, g), GROUPS)
    for y in range(9):
        part16[y] = part[y * 40 : (y + 1) * 40].astype(BF)
    copies += [
        halo(i, part16.at[pl.ds(*Y_PART[a]), pl.ds(*Z_PART[b])], pieces[i]) for i, (a, b) in enumerate(AROUND)
    ]
    pltpu.make_async_remote_copy(
        src_ref=sent.at[pl.ds(1, devices - 1)],
        dst_ref=got.at[pl.ds(1, devices - 1)],
        send_sem=out_all,
        recv_sem=in_group.at[0],
        device_id=device(0, 1),
        device_id_type=MESH,
    ).wait_send()
    for c in copies:
        c.wait()

    unet_body(
        ny, nz, me_y, me_z, part, *pieces, cext, t1, t2, t2f, t1f, b1, b2,
        wide, deep, pay, dens, act, ds1, d2, d1, g2, g1, s2, s1,
    )

    def turn():
        for y in range(8):
            refined[:, y] = jnp.swapaxes(wide[y], 0, 1).astype(BF)
            field[:, y] = jnp.swapaxes(deep[y], 0, 1)[:4]

    reduce_body(ny, nz, me_y, me_z, pay, sums, from_z, from_y, out_sum, in_sum, turn)


def whole_step(ny, nz, slots, *args):
    devices = ny * nz
    return pl.pallas_call(
        functools.partial(step_body, ny, nz),
        out_shape=[
            jax.ShapeDtypeStruct((16, 8, 8, 128), BF),
            jax.ShapeDtypeStruct((4, 8, 8, 128), F32),
            jax.ShapeDtypeStruct((ny, 16, 128), F32),
        ],
        in_specs=[VMEM] * 9,
        out_specs=[VMEM] * 3,
        scratch_shapes=[
            pltpu.VMEM((devices, 8, slots), F32),
            pltpu.VMEM((2 * devices, 5 * slots), F32),
            pltpu.VMEM((devices, 8, slots), F32),
            pltpu.VMEM((360, 128), F32),
            pltpu.VMEM((9, 40, 128), BF),
            pltpu.VMEM((12, 12, 16, 128), BF),
            pltpu.VMEM((384, 128), BF),
            pltpu.VMEM((192, 256), BF),
            pltpu.VMEM((192, 256), BF),
            pltpu.VMEM((96, 256), F32),
            pltpu.VMEM((16, 80, 128), BF),
            pltpu.VMEM((14, 16, 16, 128), BF),
            pltpu.VMEM((14, 16, 16, 128), F32),
            pltpu.VMEM((12, 12, 16, 128), BF),
            pltpu.VMEM((10, 10, 16, 128), BF),
            pltpu.VMEM((192, 256), F32),
            pltpu.VMEM((384, 128), F32),
            pltpu.VMEM((16, 128), F32),
            pltpu.VMEM((16, 128), F32),
        ]
        + [pltpu.VMEM((Y_PART[a][1], Z_PART[b][1], 128), BF) for a, b in AROUND]
        + [
            pltpu.VMEM((ny, 16, 128), F32),
            pltpu.VMEM((nz, 16, 128), F32),
            pltpu.VMEM((ny, 16, 128), F32),
            pltpu.VMEM((1, args[0].shape[1]), jnp.int32),
            pltpu.VMEM((1, args[0].shape[1]), jnp.int32),
            pltpu.VMEM((8, 8, 16, 128), F32),
            pltpu.VMEM((8, 8, 16, 128), BF),
            pltpu.VMEM((8, 8, 8, 128), F32),
            pltpu.SemaphoreType.DMA,
            pltpu.SemaphoreType.DMA((GROUPS,)),
            pltpu.SemaphoreType.DMA((16,)),
            pltpu.SemaphoreType.DMA((16,)),
            pltpu.SemaphoreType.DMA((2 * nz + ny,)),
            pltpu.SemaphoreType.DMA((2 * nz + ny,)),
            pltpu.SemaphoreType.REGULAR,
        ],
        compiler_params=pltpu.CompilerParams(collective_id=1, has_side_effects=True, vmem_limit_bytes=LIMIT),
        name="step",
    )(*args)


def local(off, mass, vel, dest, w1, b1, w2, b2, cot):
    ny, nz = lax.axis_size("gy"), lax.axis_size("gz")
    devices = ny * nz
    count = mass.shape[0]
    scale = 1.0 / math.sqrt(8 * 8 * 128 * devices)
    refined, field, sums = whole_step(
        ny,
        nz,
        2 * count // devices,
        off,
        mass.reshape(1, count),
        vel,
        dest.reshape(1, count),
        cot,
        w1.transpose(2, 3, 4, 1, 0).reshape(27, 4, 16),
        w2.transpose(2, 3, 4, 0, 1).reshape(27, 16, 16),
        b1.reshape(1, 16),
        b2.reshape(1, 16),
    )
    first, bias1, second, bias2, refined, field = finish(scale, sums, refined, field)
    return (
        refined,
        field,
        first.reshape(3, 3, 3, 4, 16).transpose(4, 3, 0, 1, 2),
        bias1.reshape(16),
        second.reshape(3, 3, 3, 16, 16).transpose(3, 4, 0, 1, 2),
        bias2.reshape(16),
    )


def solution(mesh):
    placed = (
        P(None, ("gy", "gz")),
        P(("gy", "gz")),
        P(None, ("gy", "gz")),
        P(("gy", "gz"), None),
        P(),
        P(),
        P(),
        P(),
        P(None, "gy", "gz", None),
    )
    return jax.shard_map(
        local,
        mesh=mesh,
        in_specs=placed,
        out_specs=(P(None, "gy", "gz", None), P(None, "gy", "gz", None), P(), P(), P(), P()),
        check_vma=False,
    )
```
